256 devices in a mesh: ctx: 32 (over y_hi, z, core), ch: 8 (over x, y_lo).
Axes of the slice: x: 4, y: 4 (y_hi: 2, y_lo: 2; y = y_hi * 2 + y_lo), z: 8, core: 2. Of those that a mesh axis runs over, the one named last changes fastest.
Arguments:
- activations: bfloat16 [2, 4096, 8192], P(None, 'ctx', 'ch'), may hold values from -62 to 62
- grad_in: bfloat16 [2, 4096, 8192], P(None, 'ctx', 'ch'), may hold values from -6 to 6
- gate_out: bfloat16 [3, 2, 4096, 8192], P(None, None, 'ctx', 'ch'), may hold values from -6 to 6
- gate_in: bfloat16 [3, 2, 4096, 8192], P(None, None, 'ctx', 'ch'), may hold values from -6 to 6
- filters: bfloat16 [3, 512, 128], P(None, 'ch'), may hold values from -0.5 to 0.5
Outputs:
- grad_input: bfloat16 [2, 4096, 8192], P(None, 'ctx', 'ch')
- grad_gate_out: bfloat16 [3, 2, 4096, 8192], P(None, None, 'ctx', 'ch')
- grad_gate_in: bfloat16 [3, 2, 4096, 8192], P(None, None, 'ctx', 'ch')
- grad_filters: float32 [3, 512, 128], P(None, 'ch', 'ctx')
The draws below stay inside these ranges and needn't reach their ends.
All inputs are finite; a program needn't handle non-finite values.
Results may differ from the reference program's by a relative error of at most 0.023.
Values may be sent and summed in bfloat16 or wider, within the bound.
A program may use at most 128 MiB of HBM per device.

```python
import math
import jax
import jax.numpy as jnp
from jax import lax

D = 8192
GROUP = 16
FL = 128
SEQS = 2
LAYERS = 3
LENGTH = 4096
GROUPS = 512
N_CTX = 32


def draw_activations(key, part):
    keys = jax.random.split(jax.random.fold_in(key, 11), 3)
    row_scale = jnp.exp(jax.random.uniform(keys[0], (SEQS, LENGTH, 1), jnp.float32) * math.log(10.0))
    col_scale = jnp.exp(jnp.linspace(0.0, math.log(3.0), D, dtype=jnp.float32) + jax.random.uniform(keys[1], (D,), jnp.float32) * math.log(3.4))
    base = jnp.clip(jax.random.normal(keys[2], (SEQS, LENGTH, D), jnp.float32), -6.0, 6.0)
    return (base * row_scale * col_scale / 10.0).astype(jnp.bfloat16)


def block_scale(stream_key, extent, shards, smallest, largest):
    def one(dim, parts):
        heights = jax.random.uniform(jax.random.fold_in(jax.random.fold_in(stream_key, 6), dim), (parts,), jnp.float32, smallest / len(shards), largest / len(shards))
        return jnp.repeat(jnp.exp(heights), extent[dim] // parts).reshape((-1,) + (1,) * (len(extent) - dim - 1))

    level = one(*shards[0])
    for cut in shards[1:]:
        level = level * one(*cut)
    return level


def bell_draw(key, dims, scale, bound, pieces=(), kind=jnp.bfloat16):
    entries = scale * jax.random.normal(key, dims, jnp.float32)
    if pieces:
        entries = entries * block_scale(key, dims, pieces, -0.22, 0.18)
    return jnp.clip(entries, -bound, bound).astype(kind)


def setup_inputs(seed: int = 0) -> dict:
    key_list = jax.random.split(jax.random.key(seed), 6)
    return {
        "activations": draw_activations(jax.random.fold_in(key_list[5], 71), 0),
        "grad_in": bell_draw(key_list[1], (SEQS, LENGTH, D), 1.0, 6.0, ((1, 32), (2, 8))),
        "gate_out": bell_draw(key_list[2], (LAYERS, SEQS, LENGTH, D), 1.0, 6.0, ((2, 32), (3, 8))),
        "gate_in": bell_draw(key_list[3], (LAYERS, SEQS, LENGTH, D), 1.0, 6.0, ((2, 32), (3, 8))),
        "filters": bell_draw(key_list[4], (LAYERS, GROUPS, FL), FL ** -0.5, 0.5, ((1, 8),)),
    }


def rows_of(folded):
    seq_count, length_all, width_all = folded.shape
    block_rows = length_all // (2 * N_CTX)
    blocks = folded.reshape(seq_count, N_CTX, 2, block_rows, width_all)
    leading = blocks[:, :, 0]
    trailing = blocks[:, ::-1, 1]
    return jnp.concatenate([leading, trailing], axis=1).reshape(seq_count, length_all, width_all)

def folded_of(ordered):
    seq_count, length_all, width_all = ordered.shape
    block_rows = length_all // (2 * N_CTX)
    blocks = ordered.reshape(seq_count, 2 * N_CTX, block_rows, width_all)
    leading = blocks[:, :N_CTX]
    trailing = blocks[:, N_CTX:][:, ::-1]
    return jnp.stack([leading, trailing], axis=2).reshape(seq_count, length_all, width_all)

def spread_taps(taps_group):
    return jnp.repeat(taps_group, GROUP, axis=0).T

def causal_filter(signal, spread):
    length_all = signal.shape[1]
    fft_size = length_all + FL
    spectrum = jnp.fft.rfft(signal, fft_size, axis=1) * jnp.fft.rfft(spread, fft_size, axis=0)[None]
    return jnp.fft.irfft(spectrum, fft_size, axis=1)[:, :length_all]

def reverse_filter(signal, spread):
    length_all = signal.shape[1]
    fft_size = length_all + FL
    spectrum = jnp.fft.rfft(signal, fft_size, axis=1) * jnp.conj(jnp.fft.rfft(spread, fft_size, axis=0))[None]
    return jnp.fft.irfft(spectrum, fft_size, axis=1)[:, :length_all]

def lag_sums(gradient, signal):
    length_all = signal.shape[1]
    fft_size = length_all + FL
    spectrum = jnp.conj(jnp.fft.rfft(signal, fft_size, axis=1)) * jnp.fft.rfft(gradient, fft_size, axis=1)
    lagged = jnp.fft.irfft(spectrum, fft_size, axis=1)[:, :FL]
    summed = lax.optimization_barrier(jnp.sum(lagged, axis=0))
    return lax.optimization_barrier(jnp.sum(summed.reshape(FL, GROUPS, GROUP), axis=2)).T

def reference(activations, grad_in, gate_out, gate_in, filters):
    current = activations
    saved = []
    for layer_index in range(LAYERS):
        spread = spread_taps(filters[layer_index].astype(jnp.float32))
        values = current.astype(jnp.float32)
        inverse_rms = lax.rsqrt(lax.optimization_barrier(jnp.mean(values * values, axis=2, keepdims=True)) + 1e-06)
        normed = values * inverse_rms
        inputs = (gate_in[layer_index].astype(jnp.float32) * normed).astype(jnp.bfloat16)
        inputs = lax.optimization_barrier(inputs)
        filtered = causal_filter(inputs.astype(jnp.float32), spread)
        saved.append((spread, inverse_rms, normed, inputs, filtered))
        current = (gate_out[layer_index].astype(jnp.float32) * filtered).astype(jnp.bfloat16)
        current = lax.optimization_barrier(current)
    gradient = rows_of(grad_in)
    out_grads = []
    in_grads = []
    filter_grads = []
    for layer_index in reversed(range(LAYERS)):
        spread, inverse_rms, normed, inputs, filtered = saved[layer_index]
        incoming = gradient.astype(jnp.float32)
        out_grads.append((incoming * filtered).astype(jnp.bfloat16))
        gated = (gate_out[layer_index].astype(jnp.float32) * incoming).astype(jnp.bfloat16)
        gated = lax.optimization_barrier(gated)
        gated_float = gated.astype(jnp.float32)
        spread_back = reverse_filter(gated_float, spread)
        filter_grads.append(lag_sums(gated_float, inputs.astype(jnp.float32)))
        in_grads.append((spread_back * normed).astype(jnp.bfloat16))
        grad_normed = spread_back * gate_in[layer_index].astype(jnp.float32)
        inner = lax.optimization_barrier(jnp.mean(grad_normed * normed, axis=2, keepdims=True))
        gradient = (inverse_rms * (grad_normed - normed * inner)).astype(jnp.bfloat16)
        gradient = lax.optimization_barrier(gradient)
    return (folded_of(gradient), jnp.stack(out_grads[::-1]), jnp.stack(in_grads[::-1]), jnp.stack(filter_grads[::-1]))
```

```python
import functools

import jax
import jax.numpy as jnp
from jax import lax
from jax.experimental import pallas as pl
from jax.experimental.pallas import tpu as pltpu
from jax.sharding import PartitionSpec as P

GROUP = 16
LAYERS = 3
SEQS = 2
ROWS = 128
LANES = 128
PER = LANES // GROUP
MESH = pl.DeviceIdType.MESH
F32 = jnp.float32
BF16 = jnp.bfloat16


def kernel(
    n, nh, width,
    act, gin, go_hbm, gi_hbm, filt,
    gin_out, ggo_out, ggi_out, gf_out,
    xs, go, gi, vs, vh, ux, zs, g3, gzx, gn, ggo, ggi, g0,
    taps, back, rev, fwdf, bc, bcp, acc, part, lags, fsend, frecv,
    load_sem, hs, hr, bs, br, ps, pr, pr2, fs, fr, as_, ar, ls, lr, out_sem,
):
    chunks = width // LANES
    groups = width // GROUP
    c, h = lax.axis_index("ctx"), lax.axis_index("ch")
    nxt, prv = lax.rem(c + 1, n), lax.rem(c + n - 1, n)
    has_next, has_prev = c < n - 1, c > 0
    zero_i = jnp.int32(0)

    barrier = pltpu.get_barrier_semaphore()

    def greet(cc, hh):
        pl.semaphore_signal(barrier, inc=1, device_id=(cc, hh), device_id_type=MESH)

    for o in range(1, nh):
        greet(c, lax.rem(h + o, nh))

    def greet_ctx(o, carry):
        greet(lax.rem(c + o, n), h)
        return carry

    lax.fori_loop(1, n, greet_ctx, 0)
    for o in range(1, nh):
        greet(nxt, lax.rem(h + o, nh))
        greet(prv, lax.rem(h + o, nh))

    def cols(k):
        return pl.ds(pl.multiple_of(k * LANES, LANES), LANES)

    def load(k, carry):
        pltpu.make_async_copy(act.at[:, :, cols(k)], xs.at[0, k], load_sem.at[0]).start()
        for i in range(LAYERS):
            pltpu.make_async_copy(gi_hbm.at[i, :, :, cols(k)], gi.at[i, k], load_sem.at[1 + i]).start()
        for i in range(LAYERS):
            pltpu.make_async_copy(go_hbm.at[i, :, :, cols(k)], go.at[i, k], load_sem.at[4 + i]).start()
        return carry

    lax.fori_loop(0, chunks, load, 0)

    def wait_bytes(ref, sem):
        pltpu.make_async_copy(ref, ref, sem).wait()

    row = lax.broadcasted_iota(jnp.int32, (ROWS, LANES), 0)
    col = lax.broadcasted_iota(jnp.int32, (ROWS, LANES), 1)
    flip = (row + col == ROWS - 1).astype(BF16)
    group_of = lax.rem(lax.broadcasted_iota(jnp.int32, (ROWS, 2 * LANES), 1), LANES) // GROUP
    group_row = lax.rem(lax.broadcasted_iota(jnp.int32, (1, 2 * LANES), 1), LANES) // GROUP

    for i in range(LAYERS):
        fwdf[i] = filt[i].astype(F32)
        rev[i] = jnp.dot(filt[i], flip, preferred_element_type=F32)

    def build_taps(i):
        def one(g, carry):
            line = jnp.broadcast_to(rev[i, pl.ds(g, 1), :], (ROWS, LANES))
            rolled = pltpu.roll(line, 1, 1, stride=1, stride_axis=0)
            taps[i, g, :, 0:LANES] = jnp.where(col > row, rolled, 0.0).astype(BF16)
            taps[i, g, :, LANES:] = jnp.where(col > row, 0.0, rolled).astype(BF16)
            return carry

        lax.fori_loop(0, groups, one, 0)

    def build_back(i):
        def one(g, carry):
            line = jnp.broadcast_to(fwdf[i, pl.ds(g, 1), :], (ROWS, LANES))
            rolled = pltpu.roll(line, 0, 1, stride=1, stride_axis=0)
            back[i, g, :, 0:LANES] = jnp.where(col < row, 0.0, rolled).astype(BF16)
            back[i, g, :, LANES:] = jnp.where(col < row, rolled, 0.0).astype(BF16)
            return carry

        lax.fori_loop(0, groups, one, 0)

    def halo_fwd(i, k):
        return pltpu.make_async_remote_copy(
            src_ref=vs.at[i, k], dst_ref=vh.at[i, k], send_sem=hs.at[i, k], recv_sem=hr.at[i, k],
            device_id=(nxt, h), device_id_type=MESH)

    def halo_bwd(i, k):
        return pltpu.make_async_remote_copy(
            src_ref=gzx.at[i, k, :, pl.ds(0, ROWS)], dst_ref=gzx.at[i, k, :, pl.ds(ROWS, ROWS)],
            send_sem=bs.at[i, k], recv_sem=br.at[i, k], device_id=(prv, h), device_id_type=MESH)

    def part_own(ph, o):
        return pltpu.make_async_remote_copy(
            src_ref=part.at[ph, h], dst_ref=part.at[ph, h], send_sem=ps.at[ph, o],
            recv_sem=pr.at[ph], device_id=(c, lax.rem(h + o, nh)), device_id_type=MESH)

    def part_next(ph, o):
        return pltpu.make_async_remote_copy(
            src_ref=part.at[ph, h], dst_ref=part.at[ph, nh + h], send_sem=ps.at[ph, nh + o],
            recv_sem=pr2.at[ph], device_id=(nxt, lax.rem(h + o, nh)), device_id_type=MESH)

    def share(ph, to_next):
        for s in range(SEQS):
            part[ph, h, s:s + 1, :] = jnp.sum(acc[s].T, axis=0, keepdims=True)
        for o in range(1, nh):
            part_own(ph, o).start()
        if to_next:
            @pl.when(has_next)
            def _():
                for o in range(nh):
                    part_next(ph, o).start()

    def column(line):
        return jnp.broadcast_to(line, (LANES, ROWS)).T

    def shared(ph, first):
        total = part[ph, first]
        for o in range(1, nh):
            total = total + part[ph, first + o]
        return total

    def wait_own(ph):
        wait_bytes(part.at[ph, pl.ds(0, nh - 1)], pr.at[ph])

    def inverse_of(total):
        return lax.rsqrt(total * (1.0 / (width * nh)) + 1e-06)

    def lag_copy(i, o):
        peer = lax.rem(c + o, n)
        return pltpu.make_async_remote_copy(
            src_ref=fsend.at[i, peer], dst_ref=frecv.at[i, c], send_sem=fs.at[i],
            recv_sem=fr.at[i], device_id=(peer, h), device_id_type=MESH)

    half = ROWS // 2
    def arrive(b):
        block = c if b == 0 else 2 * n - 1 - c
        target = lax.div(block, 2)
        at = pl.multiple_of(lax.rem(block, 2) * half, half)
        return target, pltpu.make_async_remote_copy(
            src_ref=gin.at[:, pl.ds(b * half, half), :], dst_ref=g3.at[:, pl.ds(at, half), :],
            send_sem=as_.at[b], recv_sem=ar.at[lax.rem(block, 2)],
            device_id=(target, h), device_id_type=MESH), pltpu.make_async_copy(
            gin.at[:, pl.ds(b * half, half), :], g3.at[:, pl.ds(at, half), :], ar.at[lax.rem(block, 2)])

    def leave(b, k):
        block = 2 * c + b
        late = lax.div(block, n)
        target = (1 - late) * block + late * (2 * n - 1 - block)
        at = pl.multiple_of(late * half, half)
        src = g0.at[k, :, pl.ds(b * half, half)]
        dst = gin_out.at[:, pl.ds(at, half), cols(k)]
        return target, pltpu.make_async_remote_copy(
            src_ref=src, dst_ref=dst, send_sem=ls.at[b, k], recv_sem=lr.at[late, k],
            device_id=(target, h), device_id_type=MESH), pltpu.make_async_copy(src, dst, lr.at[late, k])

    def both(ref4):
        return jnp.concatenate([ref4[0], ref4[1]], axis=1)

    def grouped(mats, i, k, rhs):
        out = jnp.zeros((ROWS, 2 * LANES), F32)
        for g in range(PER):
            r = jnp.dot(mats[i, k * PER + g], rhs, preferred_element_type=F32)
            out = jnp.where(group_of == g, r, out)
        return out

    build_taps(0)
    wait_bytes(xs.at[0], load_sem.at[0])
    wait_bytes(gi.at[0], load_sem.at[1])
    acc[...] = jnp.zeros_like(acc)

    def prepare(k, carry):
        x = xs[0, k].astype(F32)
        acc[...] += x * x
        vs[0, k] = (gi[0, k].astype(F32) * x).astype(BF16)
        return carry

    lax.fori_loop(0, chunks, prepare, 0)

    pl.semaphore_wait(barrier, n - 1 + 3 * (nh - 1))

    share(0, True)

    @pl.when(has_next)
    def _():
        def send(k, carry):
            halo_fwd(0, k).start()
            return carry

        lax.fori_loop(0, chunks, send, 0)

    for b in range(2):
        target, remote, local = arrive(b)

        @pl.when(target != c)
        def _():
            remote.start()

        @pl.when(target == c)
        def _():
            local.start()

    @pl.when(c == 0)
    def _():
        part[0:LAYERS, nh:] = jnp.zeros((LAYERS, nh, SEQS, ROWS), F32)

        def clear(k, carry):
            for i in range(LAYERS):
                vh[i, k] = jnp.zeros((SEQS, ROWS, LANES), BF16)
            return carry

        lax.fori_loop(0, chunks, clear, 0)

    @pl.when(c == n - 1)
    def _():
        def clear(k, carry):
            for i in range(LAYERS):
                gzx[i, k, :, ROWS:] = jnp.zeros((SEQS, ROWS, LANES), BF16)
            return carry

        lax.fori_loop(0, chunks, clear, 0)

    build_taps(1)
    for i in range(LAYERS):
        wait_bytes(go.at[i], load_sem.at[4 + i])
    for i in range(1, LAYERS):
        wait_bytes(gi.at[i], load_sem.at[1 + i])

    for i in range(LAYERS):
        if i == 1:
            build_taps(2)
        if i == 2:
            build_back(2)
        wait_own(i)

        @pl.when(has_prev)
        def _():
            wait_bytes(part.at[i, pl.ds(nh, nh)], pr2.at[i])

        own = inverse_of(shared(i, 0))
        before = inverse_of(shared(i, nh))
        for s in range(SEQS):
            bc[i, s] = column(own[s:s + 1])
            bcp[s] = column(before[s:s + 1])
        if i + 1 < LAYERS:
            acc[...] = jnp.zeros_like(acc)

        def forward(k, carry):
            @pl.when(has_prev)
            def _():
                halo_fwd(i, k).wait_recv()

            for s in range(SEQS):
                ux[i, k, s, 0:ROWS] = (vh[i, k, s].astype(F32) * bcp[s]).astype(BF16)
                ux[i, k, s, ROWS:] = (
                    gi[i, k, s].astype(F32) * (xs[i, k, s].astype(F32) * bc[i, s])).astype(BF16)
            z = grouped(taps, i, k, both(ux.at[i, k]))
            for s in range(SEQS):
                zs_part = z[:, s * LANES:(s + 1) * LANES]
                zs[i, k, s] = zs_part
                if i + 1 < LAYERS:
                    x_next = (go[i, k, s].astype(F32) * zs_part).astype(BF16)
                    xs[i + 1, k, s] = x_next
                    x_wide = x_next.astype(F32)
                    acc[s] += x_wide * x_wide
                    vs[i + 1, k, s] = (gi[i + 1, k, s].astype(F32) * x_wide).astype(BF16)
            if i + 1 < LAYERS:
                @pl.when(has_next)
                def _():
                    halo_fwd(i + 1, k).start()
            return carry

        lax.fori_loop(0, chunks, forward, 0)
        if i + 1 < LAYERS:
            share(i + 1, True)

    for b in range(2):
        wait_bytes(g3.at[:, pl.ds(b * half, half), :], ar.at[b])

    for i in reversed(range(LAYERS)):
        ph = LAYERS + i
        last = i == LAYERS - 1
        if not last:
            wait_own(LAYERS + i + 1)
            mean = shared(LAYERS + i + 1, 0) * (1.0 / (width * nh))
            for s in range(SEQS):
                bcp[s] = column(mean[s:s + 1]) * bc[i + 1, s]

        def enter(k, carry):
            for s in range(SEQS):
                if last:
                    g = g3[s, :, cols(k)].astype(F32)
                else:
                    g = (bc[i + 1, s] * (gn[k, s] - xs[i + 1, k, s].astype(F32) * bcp[s])).astype(BF16).astype(F32)
                gzx[i, k, s, 0:ROWS] = (go[i, k, s].astype(F32) * g).astype(BF16)
                ggo[i, k, s] = (g * zs[i, k, s]).astype(BF16)

            @pl.when(has_prev)
            def _():
                halo_bwd(i, k).start()

            pltpu.make_async_copy(ggo.at[i, k], ggo_out.at[i, :, :, cols(k)], out_sem.at[i]).start()
            return carry

        lax.fori_loop(0, chunks, enter, 0)

        if last:
            build_back(1)
            build_back(0)

        def diagonals(k, carry):
            grad = jnp.concatenate([gzx[i, k, 0, 0:ROWS], gzx[i, k, 1, 0:ROWS]], axis=1)
            turned = jnp.dot(flip, grad, preferred_element_type=F32)
            rhs = both(ux.at[i, k])
            for g in range(PER):
                lhs = jnp.where(group_row == g, turned, 0.0).astype(BF16)
                prod = lax.dot_general(lhs, rhs, (((1,), (1,)), ((), ())), preferred_element_type=F32)
                merged = jnp.where(row + col > ROWS - 1, prod[:, 0:LANES], prod[:, LANES:])
                rolled = pltpu.roll(merged, 1, 1, stride=1, stride_axis=0)
                lags[pl.ds(k * PER + g, 1), :] = jnp.sum(rolled, axis=0, keepdims=True)
            return carry

        lax.fori_loop(0, chunks, diagonals, 0)
        per = ROWS // n
        peer_row = lax.broadcasted_iota(jnp.int32, (n, LANES), 0)
        peer_col = lax.broadcasted_iota(jnp.int32, (n, LANES), 1)
        pieces = []
        for q in range(per):
            pick = (lax.rem(peer_col + peer_row * per + q, ROWS) == 0).astype(F32)
            pieces.append(lax.dot_general(
                pick, lags[...], (((1,), (1,)), ((), ())), preferred_element_type=F32,
                precision=lax.Precision.HIGHEST))
        lines = jnp.concatenate(pieces, axis=1)
        span = lines.shape[1] // 2
        for p in range(n):
            for r in range(2):
                fsend[i, p, r:r + 1, :] = lines[p:p + 1, r * span:(r + 1) * span]
        frecv[i, c] = fsend[i, c]

        def send_lags(o, carry):
            lag_copy(i, o).start()
            return carry

        lax.fori_loop(1, n, send_lags, 0)

        acc[...] = jnp.zeros_like(acc)

        def backward(k, carry):
            @pl.when(has_next)
            def _():
                halo_bwd(i, k).wait_recv()

            gu = grouped(back, i, k, both(gzx.at[i, k]))
            for s in range(SEQS):
                gu_part = gu[:, s * LANES:(s + 1) * LANES]
                normed = xs[i, k, s].astype(F32) * bc[i, s]
                ggi[i, k, s] = (gu_part * normed).astype(BF16)
                gn_part = gu_part * gi[i, k, s].astype(F32)
                gn[k, s] = gn_part
                acc[s] += gn_part * normed
            pltpu.make_async_copy(ggi.at[i, k], ggi_out.at[i, :, :, cols(k)], out_sem.at[LAYERS + i]).start()
            return carry

        lax.fori_loop(0, chunks, backward, 0)
        share(ph, False)

    wait_own(LAYERS)
    mean = shared(LAYERS, 0) * (1.0 / (width * nh))
    for s in range(SEQS):
        bcp[s] = column(mean[s:s + 1]) * bc[0, s]

    def finish(k, carry):
        for s in range(SEQS):
            g0[k, s] = (bc[0, s] * (gn[k, s] - xs[0, k, s].astype(F32) * bcp[s])).astype(BF16)
        for b in range(2):
            target, remote, local = leave(b, k)

            @pl.when(target != c)
            def _():
                remote.start()

            @pl.when(target == c)
            def _():
                local.start()
        return carry

    lax.fori_loop(0, chunks, finish, 0)

    for i in range(LAYERS):
        wait_bytes(frecv.at[i, pl.ds(0, n - 1)], fr.at[i])
        gf_out[i] = jnp.sum(frecv[i], axis=0)

    for i in range(LAYERS):
        wait_bytes(ggo.at[i], out_sem.at[i])
        wait_bytes(ggi.at[i], out_sem.at[LAYERS + i])
        wait_bytes(fsend.at[i, pl.ds(0, n - 1)], fs.at[i])
    for ph in range(2 * LAYERS):
        for o in range(1, nh):
            part_own(ph, o).wait_send()
    for b in range(2):
        target, remote, local = arrive(b)

        @pl.when(target != c)
        def _():
            remote.wait_send()

    @pl.when(has_next)
    def _():
        for ph in range(LAYERS):
            for o in range(nh):
                part_next(ph, o).wait_send()

        def drain(k, carry):
            for i in range(LAYERS):
                halo_fwd(i, k).wait_send()
            return carry

        lax.fori_loop(0, chunks, drain, 0)

    @pl.when(has_prev)
    def _():
        def drain(k, carry):
            for i in range(LAYERS):
                halo_bwd(i, k).wait_send()
            return carry

        lax.fori_loop(0, chunks, drain, 0)

    def drain(k, carry):
        for b in range(2):
            target, remote, local = leave(b, k)

            @pl.when(target != c)
            def _():
                remote.wait_send()

            wait_bytes(gin_out.at[:, pl.ds(b * half, half), cols(k)], lr.at[b, k])
        return carry

    lax.fori_loop(0, chunks, drain, 0)


def local(n, nh, activations, grad_in, gate_out, gate_in, filters):
    width = activations.shape[2]
    chunks, groups = width // LANES, width // GROUP
    per = ROWS // n
    span = per * groups // 2
    block = (SEQS, ROWS, LANES)
    wide = (SEQS, 2 * ROWS, LANES)
    any_spec = pl.BlockSpec(memory_space=pl.ANY)
    vmem_spec = pl.BlockSpec(memory_space=pltpu.VMEM)
    dma = pltpu.SemaphoreType.DMA
    grad_input, ggo, ggi, lags = pl.pallas_call(
        functools.partial(kernel, n, nh, width),
        out_shape=(
            jax.ShapeDtypeStruct(activations.shape, BF16),
            jax.ShapeDtypeStruct(gate_out.shape, BF16),
            jax.ShapeDtypeStruct(gate_in.shape, BF16),
            jax.ShapeDtypeStruct((LAYERS, 2, span), F32),
        ),
        in_specs=[any_spec] * 4 + [vmem_spec],
        out_specs=(any_spec, any_spec, any_spec, vmem_spec),
        scratch_shapes=[
            pltpu.VMEM((LAYERS, chunks) + block, BF16),
            pltpu.VMEM((LAYERS, chunks) + block, BF16),
            pltpu.VMEM((LAYERS, chunks) + block, BF16),
            pltpu.VMEM((LAYERS, chunks) + block, BF16),
            pltpu.VMEM((LAYERS, chunks) + block, BF16),
            pltpu.VMEM((LAYERS, chunks) + wide, BF16),
            pltpu.VMEM((LAYERS, chunks) + block, F32),
            pltpu.VMEM((SEQS, ROWS, width), BF16),
            pltpu.VMEM((LAYERS, chunks) + wide, BF16),
            pltpu.VMEM((chunks,) + block, F32),
            pltpu.VMEM((LAYERS, chunks) + block, BF16),
            pltpu.VMEM((LAYERS, chunks) + block, BF16),
            pltpu.VMEM((chunks,) + block, BF16),
            pltpu.VMEM((LAYERS, groups, ROWS, 2 * LANES), BF16),
            pltpu.VMEM((LAYERS, groups, ROWS, 2 * LANES), BF16),
            pltpu.VMEM((LAYERS, groups, LANES), F32),
            pltpu.VMEM((LAYERS, groups, LANES), F32),
            pltpu.VMEM((LAYERS,) + block, F32),
            pltpu.VMEM(block, F32),
            pltpu.VMEM(block, F32),
            pltpu.VMEM((2 * LAYERS, 2 * nh, SEQS, ROWS), F32),
            pltpu.VMEM((groups, LANES), F32),
            pltpu.VMEM((LAYERS, n, 2, span), F32),
            pltpu.VMEM((LAYERS, n, 2, span), F32),
            dma((7,)),
            dma((LAYERS, chunks)), dma((LAYERS, chunks)),
            dma((LAYERS, chunks)), dma((LAYERS, chunks)),
            dma((2 * LAYERS, 2 * nh)), dma((2 * LAYERS,)), dma((2 * LAYERS,)),
            dma((LAYERS,)), dma((LAYERS,)),
            dma((2,)), dma((2,)),
            dma((2, chunks)), dma((2, chunks)),
            dma((2 * LAYERS,)),
        ],
        compiler_params=pltpu.CompilerParams(
            collective_id=0, has_side_effects=True, vmem_limit_bytes=64 * 1024 * 1024 - 65536),
    )(activations, grad_in, gate_out, gate_in, filters)
    grad_filters = lags.reshape(LAYERS, per, groups).transpose(0, 2, 1)
    return grad_input, ggo, ggi, grad_filters


def solution(mesh):
    n, nh = mesh.shape["ctx"], mesh.shape["ch"]
    return jax.shard_map(
        functools.partial(local, n, nh),
        mesh=mesh,
        in_specs=(
            P(None, "ctx", "ch"),
            P(None, "ctx", "ch"),
            P(None, None, "ctx", "ch"),
            P(None, None, "ctx", "ch"),
            P(None, "ch", None),
        ),
        out_specs=(
            P(None, "ctx", "ch"),
            P(None, None, "ctx", "ch"),
            P(None, None, "ctx", "ch"),
            P(None, "ch", "ctx"),
        ),
        check_vma=False,
    )
```

```python
import functools

import jax
import jax.numpy as jnp
from jax import lax
from jax.experimental import pallas as pl
from jax.experimental.pallas import tpu as pltpu
from jax.sharding import PartitionSpec as P

GROUP = 16
LAYERS = 3
SEQS = 2
ROWS = 128
LANES = 128
PER = LANES // GROUP
MESH = pl.DeviceIdType.MESH
F32 = jnp.float32
BF16 = jnp.bfloat16


def kernel(
    n, nh, width,
    act, gin, go_hbm, gi_hbm, filt,
    gin_out, ggo_out, ggi_out, gf_out,
    xs, go, gi, vs, vh, ux, zs, g3, gzx, gn, ggo, ggi, g0,
    taps, back, rev, fwdf, bc, bcp, acc, part, lags, fsend, frecv,
    load_sem, hs, hr, bs, br, ps, pr, pr2, fs, fr, as_, ar, ls, lr, out_sem,
):
    chunks = width // LANES
    groups = width // GROUP
    c, h = lax.axis_index("ctx"), lax.axis_index("ch")
    nxt, prv = lax.rem(c + 1, n), lax.rem(c + n - 1, n)
    has_next, has_prev = c < n - 1, c > 0
    zero_i = jnp.int32(0)

    barrier = pltpu.get_barrier_semaphore()

    def greet(cc, hh):
        pl.semaphore_signal(barrier, inc=1, device_id=(cc, hh), device_id_type=MESH)

    for o in range(1, nh):
        greet(c, lax.rem(h + o, nh))

    def greet_ctx(o, carry):
        greet(lax.rem(c + o, n), h)
        return carry

    lax.fori_loop(1, n, greet_ctx, 0)
    for o in range(1, nh):
        greet(nxt, lax.rem(h + o, nh))
        greet(prv, lax.rem(h + o, nh))

    def cols(k):
        return pl.ds(pl.multiple_of(k * LANES, LANES), LANES)

    def load(k, carry):
        pltpu.make_async_copy(act.at[:, :, cols(k)], xs.at[0, k], load_sem.at[0]).start()
        for i in range(LAYERS):
            pltpu.make_async_copy(gi_hbm.at[i, :, :, cols(k)], gi.at[i, k], load_sem.at[1 + i]).start()
        for i in range(LAYERS):
            pltpu.make_async_copy(go_hbm.at[i, :, :, cols(k)], go.at[i, k], load_sem.at[4 + i]).start()
        return carry

    lax.fori_loop(0, chunks, load, 0)

    def wait_bytes(ref, sem):
        pltpu.make_async_copy(ref, ref, sem).wait()

    row = lax.broadcasted_iota(jnp.int32, (ROWS, LANES), 0)
    col = lax.broadcasted_iota(jnp.int32, (ROWS, LANES), 1)
    flip = (row + col == ROWS - 1).astype(BF16)
    group_of = lax.rem(lax.broadcasted_iota(jnp.int32, (ROWS, 2 * LANES), 1), LANES) // GROUP
    tiles = ROWS // 16
    own_group = (lax.broadcasted_iota(jnp.int32, (ROWS, 2 * LANES), 0) // 16 == group_of).astype(BF16)

    for i in range(LAYERS):
        fwdf[i] = filt[i].astype(F32)
        rev[i] = jnp.dot(filt[i], flip, preferred_element_type=F32)

    above = (col > row).astype(BF16)
    not_below = (col >= row).astype(BF16)

    def circulant(mats, i, lines, shift, first):
        def some(q, carry):
            for r in range(PER):
                g = q * PER + r
                line = jnp.broadcast_to(lines[i, pl.ds(g, 1), :], (16, LANES))
                base = pltpu.roll(line, shift, 1, stride=1, stride_axis=0)
                for t in range(ROWS // 16):
                    at = slice(16 * t, 16 * t + 16)
                    turn = (pltpu.roll(base, 16 * t, 1) if t else base).astype(BF16)
                    kept = turn * first[at]
                    mats[i, g, at, 0:LANES] = kept
                    mats[i, g, at, LANES:] = turn - kept
            return carry

        lax.fori_loop(0, chunks, some, 0)

    def build_taps(i):
        circulant(taps, i, rev, 1, above)

    def build_back(i):
        circulant(back, i, fwdf, 0, not_below)

    def halo_fwd(i, k):
        return pltpu.make_async_remote_copy(
            src_ref=vs.at[i, k], dst_ref=vh.at[i, k], send_sem=hs.at[i, k], recv_sem=hr.at[i, k],
            device_id=(nxt, h), device_id_type=MESH)

    def halo_bwd(i, k):
        return pltpu.make_async_remote_copy(
            src_ref=gzx.at[i, k, :, pl.ds(0, ROWS)], dst_ref=gzx.at[i, k, :, pl.ds(ROWS, ROWS)],
            send_sem=bs.at[i, k], recv_sem=br.at[i, k], device_id=(prv, h), device_id_type=MESH)

    def part_own(ph, o):
        return pltpu.make_async_remote_copy(
            src_ref=part.at[ph, h], dst_ref=part.at[ph, h], send_sem=ps.at[ph, o],
            recv_sem=pr.at[ph], device_id=(c, lax.rem(h + o, nh)), device_id_type=MESH)

    def part_next(ph, o):
        return pltpu.make_async_remote_copy(
            src_ref=part.at[ph, h], dst_ref=part.at[ph, nh + h], send_sem=ps.at[ph, nh + o],
            recv_sem=pr2.at[ph], device_id=(nxt, lax.rem(h + o, nh)), device_id_type=MESH)

    def share(ph, to_next):
        for s in range(SEQS):
            part[ph, h, s:s + 1, :] = jnp.sum(acc[s].T, axis=0, keepdims=True)
        for o in range(1, nh):
            part_own(ph, o).start()
        if to_next:
            @pl.when(has_next)
            def _():
                for o in range(nh):
                    part_next(ph, o).start()

    def column(line):
        return jnp.broadcast_to(line, (LANES, ROWS)).T

    def shared(ph, first):
        total = part[ph, first]
        for o in range(1, nh):
            total = total + part[ph, first + o]
        return total

    def wait_own(ph):
        wait_bytes(part.at[ph, pl.ds(0, nh - 1)], pr.at[ph])

    def inverse_of(total):
        return lax.rsqrt(total * (1.0 / (width * nh)) + 1e-06)

    def lag_copy(i, o):
        peer = lax.rem(c + o, n)
        return pltpu.make_async_remote_copy(
            src_ref=fsend.at[i, peer], dst_ref=frecv.at[i, c], send_sem=fs.at[i],
            recv_sem=fr.at[i], device_id=(peer, h), device_id_type=MESH)

    half = ROWS // 2
    def arrive(b, k):
        block = c if b == 0 else 2 * n - 1 - c
        target = lax.div(block, 2)
        slot = lax.rem(block, 2)
        at = pl.multiple_of(slot * half, half)
        src = gin.at[:, pl.ds(b * half, half), cols(k)]
        dst = g3.at[:, pl.ds(at, half), cols(k)]
        return target, pltpu.make_async_remote_copy(
            src_ref=src, dst_ref=dst, send_sem=as_.at[b, k], recv_sem=ar.at[slot, k],
            device_id=(target, h), device_id_type=MESH), pltpu.make_async_copy(src, dst, ar.at[slot, k])

    def leave(b, k):
        block = 2 * c + b
        late = lax.div(block, n)
        target = (1 - late) * block + late * (2 * n - 1 - block)
        at = pl.multiple_of(late * half, half)
        src = g0.at[k, :, pl.ds(b * half, half)]
        dst = gin_out.at[:, pl.ds(at, half), cols(k)]
        return target, pltpu.make_async_remote_copy(
            src_ref=src, dst_ref=dst, send_sem=ls.at[b, k], recv_sem=lr.at[late, k],
            device_id=(target, h), device_id_type=MESH), pltpu.make_async_copy(src, dst, lr.at[late, k])

    def both(ref4):
        return jnp.concatenate([ref4[0], ref4[1]], axis=1)

    def grouped(mats, i, k, rhs):
        out = jnp.zeros((ROWS, 2 * LANES), F32)
        for g in range(PER):
            r = jnp.dot(mats[i, k * PER + g], rhs, preferred_element_type=F32)
            out = jnp.where(group_of == g, r, out)
        return out

    build_taps(0)
    wait_bytes(xs.at[0], load_sem.at[0])
    wait_bytes(gi.at[0], load_sem.at[1])
    acc[...] = jnp.zeros_like(acc)

    def prepare(k, carry):
        x = xs[0, k].astype(F32)
        acc[...] += x * x
        vs[0, k] = (gi[0, k].astype(F32) * x).astype(BF16)
        return carry

    lax.fori_loop(0, chunks, prepare, 0)

    pl.semaphore_wait(barrier, n - 1 + 3 * (nh - 1))

    share(0, True)

    @pl.when(has_next)
    def _():
        def send(k, carry):
            halo_fwd(0, k).start()
            return carry

        lax.fori_loop(0, chunks, send, 0)

    @pl.when(c == 0)
    def _():
        part[0:LAYERS, nh:] = jnp.zeros((LAYERS, nh, SEQS, ROWS), F32)

        def clear(k, carry):
            for i in range(LAYERS):
                vh[i, k] = jnp.zeros((SEQS, ROWS, LANES), BF16)
            return carry

        lax.fori_loop(0, chunks, clear, 0)

    @pl.when(c == n - 1)
    def _():
        def clear(k, carry):
            for i in range(LAYERS):
                gzx[i, k, :, ROWS:] = jnp.zeros((SEQS, ROWS, LANES), BF16)
            return carry

        lax.fori_loop(0, chunks, clear, 0)

    build_taps(1)
    for i in range(LAYERS):
        wait_bytes(go.at[i], load_sem.at[4 + i])
    for i in range(1, LAYERS):
        wait_bytes(gi.at[i], load_sem.at[1 + i])

    for i in range(LAYERS):
        if i == 1:
            build_taps(2)
        if i == 2:
            build_back(2)
        wait_own(i)

        @pl.when(has_prev)
        def _():
            wait_bytes(part.at[i, pl.ds(nh, nh)], pr2.at[i])

        own = inverse_of(shared(i, 0))
        before = inverse_of(shared(i, nh))
        for s in range(SEQS):
            bc[i, s] = column(own[s:s + 1])
            bcp[s] = column(before[s:s + 1])
        if i + 1 < LAYERS:
            acc[...] = jnp.zeros_like(acc)

        def forward(k, carry):
            @pl.when(has_prev)
            def _():
                halo_fwd(i, k).wait_recv()

            for s in range(SEQS):
                ux[i, k, s, 0:ROWS] = (vh[i, k, s].astype(F32) * bcp[s]).astype(BF16)
                ux[i, k, s, ROWS:] = (
                    gi[i, k, s].astype(F32) * (xs[i, k, s].astype(F32) * bc[i, s])).astype(BF16)
            z = grouped(taps, i, k, both(ux.at[i, k]))
            for s in range(SEQS):
                zs_part = z[:, s * LANES:(s + 1) * LANES]
                zs[i, k, s] = zs_part
                if i + 1 < LAYERS:
                    x_next = (go[i, k, s].astype(F32) * zs_part).astype(BF16)
                    xs[i + 1, k, s] = x_next
                    x_wide = x_next.astype(F32)
                    acc[s] += x_wide * x_wide
                    vs[i + 1, k, s] = (gi[i + 1, k, s].astype(F32) * x_wide).astype(BF16)
            if i + 1 < LAYERS:
                @pl.when(has_next)
                def _():
                    halo_fwd(i + 1, k).start()

                target, remote, local = arrive(i, k)

                @pl.when(target != c)
                def _():
                    remote.start()

                @pl.when(target == c)
                def _():
                    local.start()
            return carry

        lax.fori_loop(0, chunks, forward, 0)
        if i + 1 < LAYERS:
            share(i + 1, True)

    early = chunks // 2
    for i in reversed(range(LAYERS)):
        ph = LAYERS + i
        last = i == LAYERS - 1
        if not last:
            wait_own(LAYERS + i + 1)
            mean = shared(LAYERS + i + 1, 0) * (1.0 / (width * nh))
            for s in range(SEQS):
                bcp[s] = column(mean[s:s + 1]) * bc[i + 1, s]

        def enter(k, carry):
            if last:
                for b in range(2):
                    wait_bytes(g3.at[:, pl.ds(b * half, half), cols(k)], ar.at[b, k])
            for s in range(SEQS):
                if last:
                    g = g3[s, :, cols(k)].astype(F32)
                else:
                    g = (bc[i + 1, s] * (gn[k, s] - xs[i + 1, k, s].astype(F32) * bcp[s])).astype(BF16).astype(F32)
                gzx[i, k, s, 0:ROWS] = (go[i, k, s].astype(F32) * g).astype(BF16)
                ggo[i, k, s] = (g * zs[i, k, s]).astype(BF16)

            @pl.when(has_prev)
            def _():
                halo_bwd(i, k).start()

            pltpu.make_async_copy(ggo.at[i, k], ggo_out.at[i, :, :, cols(k)], out_sem.at[i]).start()
            return carry

        lax.fori_loop(0, chunks, enter, 0)

        if last:
            build_back(1)
            build_back(0)

        def diagonals(k, carry):
            grad = jnp.concatenate([gzx[i, k, 0, 0:ROWS], gzx[i, k, 1, 0:ROWS]], axis=1)
            turned = jnp.dot(flip, grad, preferred_element_type=F32).astype(BF16)
            rows = both(ux.at[i, k])
            lhs, rhs = [], []
            for t in range(tiles):
                tile = turned[ROWS - 16 * t - 16:ROWS - 16 * t]
                lhs.append(jnp.concatenate([tile] * PER, axis=0) * own_group)
                rhs.append(rows[16 * t:16 * t + ROWS + 16])
            prod = lax.dot_general(
                jnp.concatenate(lhs, axis=1), jnp.concatenate(rhs, axis=1),
                (((1,), (1,)), ((), ())), preferred_element_type=F32)
            tail = jnp.concatenate([prod[:, ROWS:], jnp.zeros((ROWS, LANES - 16), F32)], axis=1)
            merged = jnp.where(col + lax.rem(row, 16) > 15, prod[:, 0:LANES], tail)
            for g in range(PER):
                rolled = pltpu.roll(merged[16 * g:16 * g + 16], LANES - 15, 1, stride=1, stride_axis=0)
                lags[pl.ds(k * PER + g, 1), :] = jnp.sum(rolled, axis=0, keepdims=True)
            return carry

        lax.fori_loop(0, early, diagonals, 0)
        acc[...] = jnp.zeros_like(acc)

        def backward(k, carry):
            @pl.when(has_next)
            def _():
                halo_bwd(i, k).wait_recv()

            gu = grouped(back, i, k, both(gzx.at[i, k]))
            for s in range(SEQS):
                gu_part = gu[:, s * LANES:(s + 1) * LANES]
                normed = xs[i, k, s].astype(F32) * bc[i, s]
                ggi[i, k, s] = (gu_part * normed).astype(BF16)
                gn_part = gu_part * gi[i, k, s].astype(F32)
                gn[k, s] = gn_part
                acc[s] += gn_part * normed
            pltpu.make_async_copy(ggi.at[i, k], ggi_out.at[i, :, :, cols(k)], out_sem.at[LAYERS + i]).start()
            return carry

        lax.fori_loop(0, chunks, backward, 0)
        share(ph, False)
        lax.fori_loop(early, chunks, diagonals, 0)
        per = ROWS // n
        peer_row = lax.broadcasted_iota(jnp.int32, (n, LANES), 0)
        peer_col = lax.broadcasted_iota(jnp.int32, (n, LANES), 1)
        pieces = []
        for q in range(per):
            pick = (lax.rem(peer_col + peer_row * per + q, ROWS) == 0).astype(F32)
            pieces.append(lax.dot_general(
                pick, lags[...], (((1,), (1,)), ((), ())), preferred_element_type=F32,
                precision=lax.Precision.HIGHEST))
        lines = jnp.concatenate(pieces, axis=1)
        span = lines.shape[1] // 2
        for p in range(n):
            for r in range(2):
                fsend[i, p, r:r + 1, :] = lines[p:p + 1, r * span:(r + 1) * span]
        frecv[i, c] = fsend[i, c]

        def send_lags(o, carry):
            lag_copy(i, o).start()
            return carry

        lax.fori_loop(1, n, send_lags, 0)

    wait_own(LAYERS)
    mean = shared(LAYERS, 0) * (1.0 / (width * nh))
    for s in range(SEQS):
        bcp[s] = column(mean[s:s + 1]) * bc[0, s]

    def finish(k, carry):
        for s in range(SEQS):
            g0[k, s] = (bc[0, s] * (gn[k, s] - xs[0, k, s].astype(F32) * bcp[s])).astype(BF16)
        for b in range(2):
            target, remote, local = leave(b, k)

            @pl.when(target != c)
            def _():
                remote.start()

            @pl.when(target == c)
            def _():
                local.start()
        return carry

    lax.fori_loop(0, chunks, finish, 0)

    for i in range(LAYERS):
        wait_bytes(frecv.at[i, pl.ds(0, n - 1)], fr.at[i])
        gf_out[i] = jnp.sum(frecv[i], axis=0)

    for i in range(LAYERS):
        wait_bytes(ggo.at[i], out_sem.at[i])
        wait_bytes(ggi.at[i], out_sem.at[LAYERS + i])
        wait_bytes(fsend.at[i, pl.ds(0, n - 1)], fs.at[i])
    for ph in range(2 * LAYERS):
        for o in range(1, nh):
            part_own(ph, o).wait_send()
    @pl.when(has_next)
    def _():
        for ph in range(LAYERS):
            for o in range(nh):
                part_next(ph, o).wait_send()

        def drain(k, carry):
            for i in range(LAYERS):
                halo_fwd(i, k).wait_send()
            return carry

        lax.fori_loop(0, chunks, drain, 0)

    @pl.when(has_prev)
    def _():
        def drain(k, carry):
            for i in range(LAYERS):
                halo_bwd(i, k).wait_send()
            return carry

        lax.fori_loop(0, chunks, drain, 0)

    def drain(k, carry):
        for b in range(2):
            for target, remote, local in (leave(b, k), arrive(b, k)):
                @pl.when(target != c)
                def _():
                    remote.wait_send()

            wait_bytes(gin_out.at[:, pl.ds(b * half, half), cols(k)], lr.at[b, k])
        return carry

    lax.fori_loop(0, chunks, drain, 0)


def hand_over(per, groups, a, b, c, d, a_out, b_out, c_out, d_out, held, get, put):
    pairs = [(a, a_out)] + [(b.at[i], b_out.at[i]) for i in range(LAYERS)]
    pairs += [(c.at[i], c_out.at[i]) for i in range(LAYERS)]
    for j, (src, _) in enumerate(pairs):
        pltpu.make_async_copy(src, held.at[j], get.at[j]).start()
    half = per // 2
    for i in range(LAYERS):
        for q in range(per):
            at = (q % half) * groups
            d_out[i, q:q + 1, :] = d[i, q // half:q // half + 1, at:at + groups]
    for j, (src, dst) in enumerate(pairs):
        pltpu.make_async_copy(src, held.at[j], get.at[j]).wait()
        pltpu.make_async_copy(held.at[j], dst, put.at[j]).start()
    for j, (src, dst) in enumerate(pairs):
        pltpu.make_async_copy(held.at[j], dst, put.at[j]).wait()


def local(n, nh, activations, grad_in, gate_out, gate_in, filters):
    width = activations.shape[2]
    chunks, groups = width // LANES, width // GROUP
    per = ROWS // n
    span = per * groups // 2
    block = (SEQS, ROWS, LANES)
    wide = (SEQS, 2 * ROWS, LANES)
    any_spec = pl.BlockSpec(memory_space=pl.ANY)
    vmem_spec = pl.BlockSpec(memory_space=pltpu.VMEM)
    dma = pltpu.SemaphoreType.DMA
    grad_input, ggo, ggi, lags = pl.pallas_call(
        functools.partial(kernel, n, nh, width),
        out_shape=(
            jax.ShapeDtypeStruct(activations.shape, BF16),
            jax.ShapeDtypeStruct(gate_out.shape, BF16),
            jax.ShapeDtypeStruct(gate_in.shape, BF16),
            jax.ShapeDtypeStruct((LAYERS, 2, span), F32),
        ),
        in_specs=[any_spec] * 4 + [vmem_spec],
        out_specs=(any_spec, any_spec, any_spec, vmem_spec),
        scratch_shapes=[
            pltpu.VMEM((LAYERS, chunks) + block, BF16),
            pltpu.VMEM((LAYERS, chunks) + block, BF16),
            pltpu.VMEM((LAYERS, chunks) + block, BF16),
            pltpu.VMEM((LAYERS, chunks) + block, BF16),
            pltpu.VMEM((LAYERS, chunks) + block, BF16),
            pltpu.VMEM((LAYERS, chunks) + wide, BF16),
            pltpu.VMEM((LAYERS, chunks) + block, F32),
            pltpu.VMEM((SEQS, ROWS, width), BF16),
            pltpu.VMEM((LAYERS, chunks) + wide, BF16),
            pltpu.VMEM((chunks,) + block, F32),
            pltpu.VMEM((LAYERS, chunks) + block, BF16),
            pltpu.VMEM((LAYERS, chunks) + block, BF16),
            pltpu.VMEM((chunks,) + block, BF16),
            pltpu.VMEM((LAYERS, groups, ROWS, 2 * LANES), BF16),
            pltpu.VMEM((LAYERS, groups, ROWS, 2 * LANES), BF16),
            pltpu.VMEM((LAYERS, groups, LANES), F32),
            pltpu.VMEM((LAYERS, groups, LANES), F32),
            pltpu.VMEM((LAYERS,) + block, F32),
            pltpu.VMEM(block, F32),
            pltpu.VMEM(block, F32),
            pltpu.VMEM((2 * LAYERS, 2 * nh, SEQS, ROWS), F32),
            pltpu.VMEM((groups, LANES), F32),
            pltpu.VMEM((LAYERS, n, 2, span), F32),
            pltpu.VMEM((LAYERS, n, 2, span), F32),
            dma((7,)),
            dma((LAYERS, chunks)), dma((LAYERS, chunks)),
            dma((LAYERS, chunks)), dma((LAYERS, chunks)),
            dma((2 * LAYERS, 2 * nh)), dma((2 * LAYERS,)), dma((2 * LAYERS,)),
            dma((LAYERS,)), dma((LAYERS,)),
            dma((2, chunks)), dma((2, chunks)),
            dma((2, chunks)), dma((2, chunks)),
            dma((2 * LAYERS,)),
        ],
        compiler_params=pltpu.CompilerParams(
            collective_id=0, has_side_effects=True, vmem_limit_bytes=64 * 1024 * 1024 - 65536),
    )(activations, grad_in, gate_out, gate_in, filters)
    grad_input, ggo, ggi, grad_filters = pl.pallas_call(
        functools.partial(hand_over, per, groups),
        out_shape=(
            jax.ShapeDtypeStruct(activations.shape, BF16),
            jax.ShapeDtypeStruct(gate_out.shape, BF16),
            jax.ShapeDtypeStruct(gate_in.shape, BF16),
            jax.ShapeDtypeStruct((LAYERS, per, groups), F32),
        ),
        in_specs=[any_spec] * 3 + [vmem_spec],
        out_specs=(any_spec, any_spec, any_spec, vmem_spec),
        scratch_shapes=[
            pltpu.VMEM((2 * LAYERS + 1,) + activations.shape, BF16),
            dma((2 * LAYERS + 1,)), dma((2 * LAYERS + 1,)),
        ],
    )(grad_input, ggo, ggi, lags)
    return grad_input, ggo, ggi, grad_filters.transpose(0, 2, 1)


def solution(mesh):
    n, nh = mesh.shape["ctx"], mesh.shape["ch"]
    return jax.shard_map(
        functools.partial(local, n, nh),
        mesh=mesh,
        in_specs=(
            P(None, "ctx", "ch"),
            P(None, "ctx", "ch"),
            P(None, None, "ctx", "ch"),
            P(None, None, "ctx", "ch"),
            P(None, "ch", None),
        ),
        out_specs=(
            P(None, "ctx", "ch"),
            P(None, None, "ctx", "ch"),
            P(None, None, "ctx", "ch"),
            P(None, "ch", "ctx"),
        ),
        check_vma=False,
    )
```

```python
import functools

import jax
import jax.numpy as jnp
from jax import lax
from jax.experimental import pallas as pl
from jax.experimental.pallas import tpu as pltpu
from jax.sharding import PartitionSpec as P

GROUP = 16
LAYERS = 3
SEQS = 2
ROWS = 128
LANES = 128
PER = LANES // GROUP
MESH = pl.DeviceIdType.MESH
ARRIVE = (1, 2)
F32 = jnp.float32
BF16 = jnp.bfloat16


def kernel(
    n, nh, width,
    act, gin, go_hbm, gi_hbm, filt,
    gin_out, ggo_out, ggi_out, gf_out,
    xs, go, gi, vs, vh, ux, zs, g3, relay, gzx, gn, ggo, ggi, g0,
    taps, back, rev, fwdf, bc, bcp, acc, part, lags, fsend, frecv,
    load_sem, hs, hr, bs, br, ps, pr, pr2, fs, fr, as_, ar, sw, ls, lr, out_sem,
):
    chunks = width // LANES
    groups = width // GROUP
    c, h = lax.axis_index("ctx"), lax.axis_index("ch")
    nxt, prv = lax.rem(c + 1, n), lax.rem(c + n - 1, n)
    has_next, has_prev = c < n - 1, c > 0
    zero_i = jnp.int32(0)

    barrier = pltpu.get_barrier_semaphore()

    def greet(cc, hh):
        pl.semaphore_signal(barrier, inc=1, device_id=(cc, hh), device_id_type=MESH)

    for o in range(1, nh):
        greet(c, lax.rem(h + o, nh))

    def greet_ctx(o, carry):
        greet(lax.rem(c + o, n), h)
        return carry

    lax.fori_loop(1, n, greet_ctx, 0)
    for o in range(1, nh):
        greet(nxt, lax.rem(h + o, nh))
        greet(prv, lax.rem(h + o, nh))

    def cols(k):
        return pl.ds(pl.multiple_of(k * LANES, LANES), LANES)

    def load(k, carry):
        pltpu.make_async_copy(act.at[:, :, cols(k)], xs.at[0, k], load_sem.at[0]).start()
        for i in range(LAYERS):
            pltpu.make_async_copy(gi_hbm.at[i, :, :, cols(k)], gi.at[i, k], load_sem.at[1 + i]).start()
        for i in range(LAYERS):
            pltpu.make_async_copy(go_hbm.at[i, :, :, cols(k)], go.at[i, k], load_sem.at[4 + i]).start()
        return carry

    lax.fori_loop(0, chunks, load, 0)

    def wait_bytes(ref, sem):
        pltpu.make_async_copy(ref, ref, sem).wait()

    row = lax.broadcasted_iota(jnp.int32, (ROWS, LANES), 0)
    col = lax.broadcasted_iota(jnp.int32, (ROWS, LANES), 1)
    flip = (row + col == ROWS - 1).astype(BF16)
    group_of = lax.rem(lax.broadcasted_iota(jnp.int32, (ROWS, 2 * LANES), 1), LANES) // GROUP
    tiles = ROWS // 16
    own_group = (lax.broadcasted_iota(jnp.int32, (ROWS, 2 * LANES), 0) // 16 == group_of).astype(BF16)

    for i in range(LAYERS):
        fwdf[i] = filt[i].astype(F32)
        rev[i] = jnp.dot(filt[i], flip, preferred_element_type=F32)

    above = (col > row).astype(BF16)
    not_below = (col >= row).astype(BF16)

    def circulant(mats, i, lines, shift, first):
        def some(q, carry):
            for r in range(PER):
                g = q * PER + r
                line = jnp.broadcast_to(lines[i, pl.ds(g, 1), :], (16, LANES))
                base = pltpu.roll(line, shift, 1, stride=1, stride_axis=0)
                for t in range(ROWS // 16):
                    at = slice(16 * t, 16 * t + 16)
                    turn = (pltpu.roll(base, 16 * t, 1) if t else base).astype(BF16)
                    kept = turn * first[at]
                    mats[i, g, at, 0:LANES] = kept
                    mats[i, g, at, LANES:] = turn - kept
            return carry

        lax.fori_loop(0, chunks, some, 0)

    def build_taps(i):
        circulant(taps, i, rev, 1, above)

    def build_back(i):
        circulant(back, i, fwdf, 0, not_below)

    def halo_fwd(i, k):
        return pltpu.make_async_remote_copy(
            src_ref=vs.at[i, k], dst_ref=vh.at[i, k], send_sem=hs.at[i, k], recv_sem=hr.at[i, k],
            device_id=(nxt, h), device_id_type=MESH)

    def halo_bwd(i, k):
        return pltpu.make_async_remote_copy(
            src_ref=gzx.at[i, k, :, pl.ds(0, ROWS)], dst_ref=gzx.at[i, k, :, pl.ds(ROWS, ROWS)],
            send_sem=bs.at[i, k], recv_sem=br.at[i, k], device_id=(prv, h), device_id_type=MESH)

    def part_own(ph, o):
        return pltpu.make_async_remote_copy(
            src_ref=part.at[ph, h], dst_ref=part.at[ph, h], send_sem=ps.at[ph, o],
            recv_sem=pr.at[ph], device_id=(c, lax.rem(h + o, nh)), device_id_type=MESH)

    def part_next(ph, o):
        return pltpu.make_async_remote_copy(
            src_ref=part.at[ph, h], dst_ref=part.at[ph, nh + h], send_sem=ps.at[ph, nh + o],
            recv_sem=pr2.at[ph], device_id=(nxt, lax.rem(h + o, nh)), device_id_type=MESH)

    def share(ph, to_next):
        for s in range(SEQS):
            part[ph, h, s:s + 1, :] = jnp.sum(acc[s].T, axis=0, keepdims=True)
        for o in range(1, nh):
            part_own(ph, o).start()
        if to_next:
            @pl.when(has_next)
            def _():
                for o in range(nh):
                    part_next(ph, o).start()

    def column(line):
        return jnp.broadcast_to(line, (LANES, ROWS)).T

    def shared(ph, first):
        total = part[ph, first]
        for o in range(1, nh):
            total = total + part[ph, first + o]
        return total

    def wait_own(ph):
        wait_bytes(part.at[ph, pl.ds(0, nh - 1)], pr.at[ph])

    def inverse_of(total):
        return lax.rsqrt(total * (1.0 / (width * nh)) + 1e-06)

    def lag_copy(i, o):
        peer = lax.rem(c + o, n)
        return pltpu.make_async_remote_copy(
            src_ref=fsend.at[i, peer], dst_ref=frecv.at[i, c], send_sem=fs.at[i],
            recv_sem=fr.at[i], device_id=(peer, h), device_id_type=MESH)

    half = ROWS // 2
    side = lax.div(c, lax.div(n, 2))
    near = c - side * lax.div(n, 2)
    chip = lax.div(near, 2)
    trade = (3 * n // 8 if n == 32 else 0) * (
        lax.div(7 - chip, 7) - lax.div(36 - (chip - 6) * (chip - 6), 36))
    give_to = (1 - side) * (c + lax.div(n, 2)) + side * (near + trade)
    across = (1 - side) * (c + trade + lax.div(n, 2)) + side * near

    def swap():
        return pltpu.make_async_remote_copy(
            src_ref=gin.at[:, pl.ds(pl.multiple_of((1 - side) * half, half), half), :], dst_ref=relay,
            send_sem=sw.at[0], recv_sem=sw.at[1], device_id=(give_to, h), device_id_type=MESH)

    def arrive(b, k):
        source = c if b == 0 else across
        block = source + side * (2 * n - 1 - 2 * source)
        target = lax.div(block, 2)
        slot = lax.rem(block, 2)
        at = pl.multiple_of(slot * half, half)
        src = gin.at[:, pl.ds(pl.multiple_of(side * half, half), half), cols(k)] if b == 0 else relay.at[:, :, cols(k)]
        dst = g3.at[:, pl.ds(at, half), cols(k)]
        return target, pltpu.make_async_remote_copy(
            src_ref=src, dst_ref=dst, send_sem=as_.at[b, k], recv_sem=ar.at[slot, k],
            device_id=(target, h), device_id_type=MESH), pltpu.make_async_copy(src, dst, ar.at[slot, k])

    def send_arrive(b):
        if b == 1:
            swap().wait_recv()

        def some(k, carry):
            target, remote, local = arrive(b, k)

            @pl.when(target != c)
            def _():
                remote.start()

            @pl.when(target == c)
            def _():
                local.start()
            return carry

        lax.fori_loop(0, chunks, some, 0)

    def leave(b, k):
        block = 2 * c + b
        late = lax.div(block, n)
        target = (1 - late) * block + late * (2 * n - 1 - block)
        at = pl.multiple_of(late * half, half)
        src = g0.at[k, :, pl.ds(b * half, half)]
        dst = gin_out.at[:, pl.ds(at, half), cols(k)]
        return target, pltpu.make_async_remote_copy(
            src_ref=src, dst_ref=dst, send_sem=ls.at[b, k], recv_sem=lr.at[late, k],
            device_id=(target, h), device_id_type=MESH), pltpu.make_async_copy(src, dst, lr.at[late, k])

    def both(ref4):
        return jnp.concatenate([ref4[0], ref4[1]], axis=1)

    def grouped(mats, i, k, rhs):
        out = jnp.zeros((ROWS, 2 * LANES), F32)
        for g in range(PER):
            r = jnp.dot(mats[i, k * PER + g], rhs, preferred_element_type=F32)
            out = jnp.where(group_of == g, r, out)
        return out

    build_taps(0)
    wait_bytes(xs.at[0], load_sem.at[0])
    wait_bytes(gi.at[0], load_sem.at[1])
    acc[...] = jnp.zeros_like(acc)

    def prepare(k, carry):
        x = xs[0, k].astype(F32)
        acc[...] += x * x
        vs[0, k] = (gi[0, k].astype(F32) * x).astype(BF16)
        return carry

    lax.fori_loop(0, chunks, prepare, 0)

    pl.semaphore_wait(barrier, n - 1 + 3 * (nh - 1))

    share(0, True)

    @pl.when(has_next)
    def _():
        def send(k, carry):
            halo_fwd(0, k).start()
            return carry

        lax.fori_loop(0, chunks, send, 0)

    @pl.when(c == 0)
    def _():
        part[0:LAYERS, nh:] = jnp.zeros((LAYERS, nh, SEQS, ROWS), F32)

        def clear(k, carry):
            for i in range(LAYERS):
                vh[i, k] = jnp.zeros((SEQS, ROWS, LANES), BF16)
            return carry

        lax.fori_loop(0, chunks, clear, 0)

    @pl.when(c == n - 1)
    def _():
        def clear(k, carry):
            for i in range(LAYERS):
                gzx[i, k, :, ROWS:] = jnp.zeros((SEQS, ROWS, LANES), BF16)
            return carry

        lax.fori_loop(0, chunks, clear, 0)

    swap().start()
    if 0 in ARRIVE:
        send_arrive(ARRIVE.index(0))
    build_taps(1)
    for i in range(LAYERS):
        wait_bytes(go.at[i], load_sem.at[4 + i])
    for i in range(1, LAYERS):
        wait_bytes(gi.at[i], load_sem.at[1 + i])

    step = 2 if chunks % 2 == 0 else 1
    for i in range(LAYERS):
        if i == 1:
            build_taps(2)
        if i == 2:
            build_back(2)
        wait_own(i)

        @pl.when(has_prev)
        def _():
            wait_bytes(part.at[i, pl.ds(nh, nh)], pr2.at[i])

        own = inverse_of(shared(i, 0))
        before = inverse_of(shared(i, nh))
        for s in range(SEQS):
            bc[i, s] = column(own[s:s + 1])
            bcp[s] = column(before[s:s + 1])
        if i + 1 < LAYERS:
            acc[...] = jnp.zeros_like(acc)

        def forward_one(k):
            for s in range(SEQS):
                ux[i, k, s, 0:ROWS] = (vh[i, k, s].astype(F32) * bcp[s]).astype(BF16)
                ux[i, k, s, ROWS:] = (
                    gi[i, k, s].astype(F32) * (xs[i, k, s].astype(F32) * bc[i, s])).astype(BF16)
            z = grouped(taps, i, k, both(ux.at[i, k]))
            for s in range(SEQS):
                zs_part = z[:, s * LANES:(s + 1) * LANES]
                zs[i, k, s] = zs_part
                if i + 1 < LAYERS:
                    x_next = (go[i, k, s].astype(F32) * zs_part).astype(BF16)
                    xs[i + 1, k, s] = x_next
                    x_wide = x_next.astype(F32)
                    acc[s] += x_wide * x_wide
                    vs[i + 1, k, s] = (gi[i + 1, k, s].astype(F32) * x_wide).astype(BF16)

        def forward(q, carry):
            ks = [q * step + r for r in range(step)]

            @pl.when(has_prev)
            def _():
                for k in ks:
                    halo_fwd(i, k).wait_recv()

            for k in ks:
                forward_one(k)
            if i + 1 < LAYERS:
                @pl.when(has_next)
                def _():
                    for k in ks:
                        halo_fwd(i + 1, k).start()
            return carry

        lax.fori_loop(0, chunks // step, forward, 0)
        if i + 1 < LAYERS:
            share(i + 1, True)
            if i + 1 in ARRIVE:
                send_arrive(ARRIVE.index(i + 1))

    early = chunks // 2
    for i in reversed(range(LAYERS)):
        ph = LAYERS + i
        last = i == LAYERS - 1
        if not last:
            wait_own(LAYERS + i + 1)
            mean = shared(LAYERS + i + 1, 0) * (1.0 / (width * nh))
            for s in range(SEQS):
                bcp[s] = column(mean[s:s + 1]) * bc[i + 1, s]

        def enter(k, carry):
            if last:
                for b in range(2):
                    wait_bytes(g3.at[:, pl.ds(b * half, half), cols(k)], ar.at[b, k])
            for s in range(SEQS):
                if last:
                    g = g3[s, :, cols(k)].astype(F32)
                else:
                    g = (bc[i + 1, s] * (gn[k, s] - xs[i + 1, k, s].astype(F32) * bcp[s])).astype(BF16).astype(F32)
                gzx[i, k, s, 0:ROWS] = (go[i, k, s].astype(F32) * g).astype(BF16)
                ggo[i, k, s] = (g * zs[i, k, s]).astype(BF16)

            @pl.when(has_prev)
            def _():
                halo_bwd(i, k).start()

            pltpu.make_async_copy(ggo.at[i, k], ggo_out.at[i, :, :, cols(k)], out_sem.at[i]).start()
            return carry

        lax.fori_loop(0, chunks, enter, 0)

        if last:
            build_back(1)
            build_back(0)

        def diagonals(k, carry):
            grad = jnp.concatenate([gzx[i, k, 0, 0:ROWS], gzx[i, k, 1, 0:ROWS]], axis=1)
            turned = jnp.dot(flip, grad, preferred_element_type=F32).astype(BF16)
            rows = both(ux.at[i, k])
            lhs, rhs = [], []
            for t in range(tiles):
                tile = turned[ROWS - 16 * t - 16:ROWS - 16 * t]
                lhs.append(jnp.concatenate([tile] * PER, axis=0) * own_group)
                rhs.append(rows[16 * t:16 * t + ROWS + 16])
            prod = lax.dot_general(
                jnp.concatenate(lhs, axis=1), jnp.concatenate(rhs, axis=1),
                (((1,), (1,)), ((), ())), preferred_element_type=F32)
            tail = jnp.concatenate([prod[:, ROWS:], jnp.zeros((ROWS, LANES - 16), F32)], axis=1)
            merged = jnp.where(col + lax.rem(row, 16) > 15, prod[:, 0:LANES], tail)
            for g in range(PER):
                rolled = pltpu.roll(merged[16 * g:16 * g + 16], LANES - 15, 1, stride=1, stride_axis=0)
                lags[pl.ds(k * PER + g, 1), :] = jnp.sum(rolled, axis=0, keepdims=True)
            return carry

        lax.fori_loop(0, early, diagonals, 0)
        acc[...] = jnp.zeros_like(acc)

        def backward_one(k):
            gu = grouped(back, i, k, both(gzx.at[i, k]))
            for s in range(SEQS):
                gu_part = gu[:, s * LANES:(s + 1) * LANES]
                normed = xs[i, k, s].astype(F32) * bc[i, s]
                ggi[i, k, s] = (gu_part * normed).astype(BF16)
                gn_part = gu_part * gi[i, k, s].astype(F32)
                gn[k, s] = gn_part
                acc[s] += gn_part * normed

        def backward(q, carry):
            ks = [q * step + r for r in range(step)]

            @pl.when(has_next)
            def _():
                for k in ks:
                    halo_bwd(i, k).wait_recv()

            for k in ks:
                backward_one(k)
            for k in ks:
                pltpu.make_async_copy(ggi.at[i, k], ggi_out.at[i, :, :, cols(k)], out_sem.at[LAYERS + i]).start()
            return carry

        lax.fori_loop(0, chunks // step, backward, 0)
        share(ph, False)
        lax.fori_loop(early, chunks, diagonals, 0)
        per = ROWS // n
        peer_row = lax.broadcasted_iota(jnp.int32, (n, LANES), 0)
        peer_col = lax.broadcasted_iota(jnp.int32, (n, LANES), 1)
        pieces = []
        for q in range(per):
            pick = (lax.rem(peer_col + peer_row * per + q, ROWS) == 0).astype(F32)
            pieces.append(lax.dot_general(
                pick, lags[...], (((1,), (1,)), ((), ())), preferred_element_type=F32,
                precision=lax.Precision.HIGHEST))
        lines = jnp.concatenate(pieces, axis=1)
        span = lines.shape[1] // 2
        for p in range(n):
            for r in range(2):
                fsend[i, p, r:r + 1, :] = lines[p:p + 1, r * span:(r + 1) * span]
        frecv[i, c] = fsend[i, c]

        def send_lags(o, carry):
            lag_copy(i, o).start()
            return carry

        lax.fori_loop(1, n, send_lags, 0)

    wait_own(LAYERS)
    mean = shared(LAYERS, 0) * (1.0 / (width * nh))
    for s in range(SEQS):
        bcp[s] = column(mean[s:s + 1]) * bc[0, s]

    def finish(k, carry):
        for s in range(SEQS):
            g0[k, s] = (bc[0, s] * (gn[k, s] - xs[0, k, s].astype(F32) * bcp[s])).astype(BF16)
        for b in range(2):
            target, remote, local = leave(b, k)

            @pl.when(target != c)
            def _():
                remote.start()

            @pl.when(target == c)
            def _():
                local.start()
        return carry

    lax.fori_loop(0, chunks, finish, 0)

    for i in range(LAYERS):
        wait_bytes(frecv.at[i, pl.ds(0, n - 1)], fr.at[i])
        gf_out[i] = jnp.sum(frecv[i], axis=0)

    swap().wait_send()
    for i in range(LAYERS):
        wait_bytes(ggo.at[i], out_sem.at[i])
        wait_bytes(ggi.at[i], out_sem.at[LAYERS + i])
        wait_bytes(fsend.at[i, pl.ds(0, n - 1)], fs.at[i])
    for ph in range(2 * LAYERS):
        for o in range(1, nh):
            part_own(ph, o).wait_send()
    @pl.when(has_next)
    def _():
        for ph in range(LAYERS):
            for o in range(nh):
                part_next(ph, o).wait_send()

        def drain(k, carry):
            for i in range(LAYERS):
                halo_fwd(i, k).wait_send()
            return carry

        lax.fori_loop(0, chunks, drain, 0)

    @pl.when(has_prev)
    def _():
        def drain(k, carry):
            for i in range(LAYERS):
                halo_bwd(i, k).wait_send()
            return carry

        lax.fori_loop(0, chunks, drain, 0)

    def drain(k, carry):
        for b in range(2):
            for target, remote, local in (leave(b, k), arrive(b, k)):
                @pl.when(target != c)
                def _():
                    remote.wait_send()

            wait_bytes(gin_out.at[:, pl.ds(b * half, half), cols(k)], lr.at[b, k])
        return carry

    lax.fori_loop(0, chunks, drain, 0)


def hand_over(per, groups, a, b, c, d, a_out, b_out, c_out, d_out, held, get, put):
    pairs = [(a, a_out)] + [(b.at[i], b_out.at[i]) for i in range(LAYERS)]
    pairs += [(c.at[i], c_out.at[i]) for i in range(LAYERS)]
    for j, (src, _) in enumerate(pairs):
        pltpu.make_async_copy(src, held.at[j], get.at[j]).start()
    half = per // 2
    for i in range(LAYERS):
        for q in range(per):
            at = (q % half) * groups
            d_out[i, q:q + 1, :] = d[i, q // half:q // half + 1, at:at + groups]
    for j, (src, dst) in enumerate(pairs):
        pltpu.make_async_copy(src, held.at[j], get.at[j]).wait()
        pltpu.make_async_copy(held.at[j], dst, put.at[j]).start()
    for j, (src, dst) in enumerate(pairs):
        pltpu.make_async_copy(held.at[j], dst, put.at[j]).wait()


def local(n, nh, activations, grad_in, gate_out, gate_in, filters):
    width = activations.shape[2]
    chunks, groups = width // LANES, width // GROUP
    per = ROWS // n
    span = per * groups // 2
    block = (SEQS, ROWS, LANES)
    wide = (SEQS, 2 * ROWS, LANES)
    any_spec = pl.BlockSpec(memory_space=pl.ANY)
    vmem_spec = pl.BlockSpec(memory_space=pltpu.VMEM)
    dma = pltpu.SemaphoreType.DMA
    grad_input, ggo, ggi, lags = pl.pallas_call(
        functools.partial(kernel, n, nh, width),
        out_shape=(
            jax.ShapeDtypeStruct(activations.shape, BF16),
            jax.ShapeDtypeStruct(gate_out.shape, BF16),
            jax.ShapeDtypeStruct(gate_in.shape, BF16),
            jax.ShapeDtypeStruct((LAYERS, 2, span), F32),
        ),
        in_specs=[any_spec] * 4 + [vmem_spec],
        out_specs=(any_spec, any_spec, any_spec, vmem_spec),
        scratch_shapes=[
            pltpu.VMEM((LAYERS, chunks) + block, BF16),
            pltpu.VMEM((LAYERS, chunks) + block, BF16),
            pltpu.VMEM((LAYERS, chunks) + block, BF16),
            pltpu.VMEM((LAYERS, chunks) + block, BF16),
            pltpu.VMEM((LAYERS, chunks) + block, BF16),
            pltpu.VMEM((LAYERS, chunks) + wide, BF16),
            pltpu.VMEM((LAYERS, chunks) + block, F32),
            pltpu.VMEM((SEQS, ROWS, width), BF16),
            pltpu.VMEM((SEQS, ROWS // 2, width), BF16),
            pltpu.VMEM((LAYERS, chunks) + wide, BF16),
            pltpu.VMEM((chunks,) + block, F32),
            pltpu.VMEM((LAYERS, chunks) + block, BF16),
            pltpu.VMEM((LAYERS, chunks) + block, BF16),
            pltpu.VMEM((chunks,) + block, BF16),
            pltpu.VMEM((LAYERS, groups, ROWS, 2 * LANES), BF16),
            pltpu.VMEM((LAYERS, groups, ROWS, 2 * LANES), BF16),
            pltpu.VMEM((LAYERS, groups, LANES), F32),
            pltpu.VMEM((LAYERS, groups, LANES), F32),
            pltpu.VMEM((LAYERS,) + block, F32),
            pltpu.VMEM(block, F32),
            pltpu.VMEM(block, F32),
            pltpu.VMEM((2 * LAYERS, 2 * nh, SEQS, ROWS), F32),
            pltpu.VMEM((groups, LANES), F32),
            pltpu.VMEM((LAYERS, n, 2, span), F32),
            pltpu.VMEM((LAYERS, n, 2, span), F32),
            dma((7,)),
            dma((LAYERS, chunks)), dma((LAYERS, chunks)),
            dma((LAYERS, chunks)), dma((LAYERS, chunks)),
            dma((2 * LAYERS, 2 * nh)), dma((2 * LAYERS,)), dma((2 * LAYERS,)),
            dma((LAYERS,)), dma((LAYERS,)),
            dma((2, chunks)), dma((2, chunks)), dma((2,)),
            dma((2, chunks)), dma((2, chunks)),
            dma((2 * LAYERS,)),
        ],
        compiler_params=pltpu.CompilerParams(
            collective_id=0, has_side_effects=True, vmem_limit_bytes=64 * 1024 * 1024 - 65536),
    )(activations, grad_in, gate_out, gate_in, filters)
    grad_input, ggo, ggi, grad_filters = pl.pallas_call(
        functools.partial(hand_over, per, groups),
        out_shape=(
            jax.ShapeDtypeStruct(activations.shape, BF16),
            jax.ShapeDtypeStruct(gate_out.shape, BF16),
            jax.ShapeDtypeStruct(gate_in.shape, BF16),
            jax.ShapeDtypeStruct((LAYERS, per, groups), F32),
        ),
        in_specs=[any_spec] * 3 + [vmem_spec],
        out_specs=(any_spec, any_spec, any_spec, vmem_spec),
        scratch_shapes=[
            pltpu.VMEM((2 * LAYERS + 1,) + activations.shape, BF16),
            dma((2 * LAYERS + 1,)), dma((2 * LAYERS + 1,)),
        ],
    )(grad_input, ggo, ggi, lags)
    return grad_input, ggo, ggi, grad_filters.transpose(0, 2, 1)


def solution(mesh):
    n, nh = mesh.shape["ctx"], mesh.shape["ch"]
    return jax.shard_map(
        functools.partial(local, n, nh),
        mesh=mesh,
        in_specs=(
            P(None, "ctx", "ch"),
            P(None, "ctx", "ch"),
            P(None, None, "ctx", "ch"),
            P(None, None, "ctx", "ch"),
            P(None, "ch", None),
        ),
        out_specs=(
            P(None, "ctx", "ch"),
            P(None, None, "ctx", "ch"),
            P(None, None, "ctx", "ch"),
            P(None, "ch", "ctx"),
        ),
        check_vma=False,
    )
```

```python
import functools

import jax
import jax.numpy as jnp
from jax import lax
from jax.experimental import pallas as pl
from jax.experimental.pallas import tpu as pltpu
from jax.sharding import PartitionSpec as P

GROUP = 16
LAYERS = 3
SEQS = 2
ROWS = 128
LANES = 128
PER = LANES // GROUP
MESH = pl.DeviceIdType.MESH
ARRIVE = (1, 2)
F32 = jnp.float32
BF16 = jnp.bfloat16


def kernel(
    n, nh, width,
    act, gin, go_hbm, gi_hbm, filt,
    gin_out, ggo_out, ggi_out, gf_out,
    xs, go, gi, vs, vh, ux, zs, g3, relay, gzx, gn, ggo, ggi, g0,
    taps, back, rev, fwdf, bc, bcp, acc, part, lags, fsend, frecv,
    load_sem, hs, hr, bs, br, ps, pr, pr2, fs, fr, as_, ar, sw, ls, lr, out_sem,
):
    chunks = width // LANES
    groups = width // GROUP
    c, h = lax.axis_index("ctx"), lax.axis_index("ch")
    nxt, prv = lax.rem(c + 1, n), lax.rem(c + n - 1, n)
    has_next, has_prev = c < n - 1, c > 0
    zero_i = jnp.int32(0)

    barrier = pltpu.get_barrier_semaphore()

    def greet(cc, hh):
        pl.semaphore_signal(barrier, inc=1, device_id=(cc, hh), device_id_type=MESH)

    for o in range(1, nh):
        greet(c, lax.rem(h + o, nh))

    def greet_ctx(o, carry):
        greet(lax.rem(c + o, n), h)
        return carry

    lax.fori_loop(1, n, greet_ctx, 0)
    for o in range(1, nh):
        greet(nxt, lax.rem(h + o, nh))
        greet(prv, lax.rem(h + o, nh))

    def cols(k):
        return pl.ds(pl.multiple_of(k * LANES, LANES), LANES)

    def load(k, carry):
        pltpu.make_async_copy(act.at[:, :, cols(k)], xs.at[0, k], load_sem.at[0]).start()
        for i in range(LAYERS):
            pltpu.make_async_copy(gi_hbm.at[i, :, :, cols(k)], gi.at[i, k], load_sem.at[1 + i]).start()
        for i in range(LAYERS):
            pltpu.make_async_copy(go_hbm.at[i, :, :, cols(k)], go.at[i, k], load_sem.at[4 + i]).start()
        return carry

    lax.fori_loop(0, chunks, load, 0)

    def wait_bytes(ref, sem):
        pltpu.make_async_copy(ref, ref, sem).wait()

    row = lax.broadcasted_iota(jnp.int32, (ROWS, LANES), 0)
    col = lax.broadcasted_iota(jnp.int32, (ROWS, LANES), 1)
    flip = (row + col == ROWS - 1).astype(BF16)
    group_of = lax.rem(lax.broadcasted_iota(jnp.int32, (ROWS, 2 * LANES), 1), LANES) // GROUP
    tiles = ROWS // 16
    own_group = (lax.broadcasted_iota(jnp.int32, (ROWS, 2 * LANES), 0) // 16 == group_of).astype(BF16)

    for i in range(LAYERS):
        fwdf[i] = filt[i].astype(F32)
        rev[i] = jnp.dot(filt[i], flip, preferred_element_type=F32)

    above = (col > row).astype(BF16)
    not_below = (col >= row).astype(BF16)

    def circulant(mats, i, lines, shift, first):
        def some(q, carry):
            for r in range(PER):
                g = q * PER + r
                line = jnp.broadcast_to(lines[i, pl.ds(g, 1), :], (16, LANES))
                base = pltpu.roll(line, shift, 1, stride=1, stride_axis=0)
                for t in range(ROWS // 16):
                    at = slice(16 * t, 16 * t + 16)
                    turn = (pltpu.roll(base, 16 * t, 1) if t else base).astype(BF16)
                    kept = turn * first[at]
                    mats[i, g, at, 0:LANES] = kept
                    mats[i, g, at, LANES:] = turn - kept
            return carry

        lax.fori_loop(0, chunks, some, 0)

    def build_taps(i):
        circulant(taps, i, rev, 1, above)

    def build_back(i):
        circulant(back, i, fwdf, 0, not_below)

    def halo_fwd(i, k):
        return pltpu.make_async_remote_copy(
            src_ref=vs.at[i, k], dst_ref=vh.at[i, k], send_sem=hs.at[i, k], recv_sem=hr.at[i, k],
            device_id=(nxt, h), device_id_type=MESH)

    def halo_bwd(i, k):
        return pltpu.make_async_remote_copy(
            src_ref=gzx.at[i, k, :, pl.ds(0, ROWS)], dst_ref=gzx.at[i, k, :, pl.ds(ROWS, ROWS)],
            send_sem=bs.at[i, k], recv_sem=br.at[i, k], device_id=(prv, h), device_id_type=MESH)

    def part_own(ph, o):
        return pltpu.make_async_remote_copy(
            src_ref=part.at[ph, h], dst_ref=part.at[ph, h], send_sem=ps.at[ph, o],
            recv_sem=pr.at[ph], device_id=(c, lax.rem(h + o, nh)), device_id_type=MESH)

    def part_next(ph, o):
        return pltpu.make_async_remote_copy(
            src_ref=part.at[ph, h], dst_ref=part.at[ph, nh + h], send_sem=ps.at[ph, nh + o],
            recv_sem=pr2.at[ph], device_id=(nxt, lax.rem(h + o, nh)), device_id_type=MESH)

    def share(ph, to_next):
        for s in range(SEQS):
            part[ph, h, s:s + 1, :] = jnp.sum(acc[s].T, axis=0, keepdims=True)
        for o in range(1, nh):
            part_own(ph, o).start()
        if to_next:
            @pl.when(has_next)
            def _():
                for o in range(nh):
                    part_next(ph, o).start()

    def column(line):
        return jnp.broadcast_to(line, (LANES, ROWS)).T

    def shared(ph, first):
        total = part[ph, first]
        for o in range(1, nh):
            total = total + part[ph, first + o]
        return total

    def wait_own(ph):
        wait_bytes(part.at[ph, pl.ds(0, nh - 1)], pr.at[ph])

    def inverse_of(total):
        return lax.rsqrt(total * (1.0 / (width * nh)) + 1e-06)

    def lag_copy(i, o):
        peer = lax.rem(c + o, n)
        return pltpu.make_async_remote_copy(
            src_ref=fsend.at[i, peer], dst_ref=frecv.at[i, c], send_sem=fs.at[i],
            recv_sem=fr.at[i], device_id=(peer, h), device_id_type=MESH)

    half = ROWS // 2
    side = lax.div(c, lax.div(n, 2))
    near = c - side * lax.div(n, 2)
    chip = lax.div(near, 2)
    trade = (3 * n // 8 if n == 32 else 0) * (
        lax.div(7 - chip, 7) - lax.div(36 - (chip - 6) * (chip - 6), 36))
    give_to = (1 - side) * (c + lax.div(n, 2)) + side * (near + trade)
    across = (1 - side) * (c + trade + lax.div(n, 2)) + side * near

    def swap():
        return pltpu.make_async_remote_copy(
            src_ref=gin.at[:, pl.ds(pl.multiple_of((1 - side) * half, half), half), :], dst_ref=relay,
            send_sem=sw.at[0], recv_sem=sw.at[1], device_id=(give_to, h), device_id_type=MESH)

    def arrive(b, k):
        source = c if b == 0 else across
        block = source + side * (2 * n - 1 - 2 * source)
        target = lax.div(block, 2)
        slot = lax.rem(block, 2)
        at = pl.multiple_of(slot * half, half)
        src = gin.at[:, pl.ds(pl.multiple_of(side * half, half), half), cols(k)] if b == 0 else relay.at[:, :, cols(k)]
        dst = g3.at[:, pl.ds(at, half), cols(k)]
        return target, pltpu.make_async_remote_copy(
            src_ref=src, dst_ref=dst, send_sem=as_.at[b, k], recv_sem=ar.at[slot, k],
            device_id=(target, h), device_id_type=MESH), pltpu.make_async_copy(src, dst, ar.at[slot, k])

    def send_arrive(b):
        if b == 1:
            swap().wait_recv()

        def some(k, carry):
            target, remote, local = arrive(b, k)

            @pl.when(target != c)
            def _():
                remote.start()

            @pl.when(target == c)
            def _():
                local.start()
            return carry

        lax.fori_loop(0, chunks, some, 0)

    def leave(b, k):
        block = 2 * c + b
        late = lax.div(block, n)
        target = (1 - late) * block + late * (2 * n - 1 - block)
        at = pl.multiple_of(late * half, half)
        src = g0.at[k, :, pl.ds(b * half, half)]
        dst = gin_out.at[:, pl.ds(at, half), cols(k)]
        return target, pltpu.make_async_remote_copy(
            src_ref=src, dst_ref=dst, send_sem=ls.at[b, k], recv_sem=lr.at[late, k],
            device_id=(target, h), device_id_type=MESH), pltpu.make_async_copy(src, dst, lr.at[late, k])

    def both(ref4):
        return jnp.concatenate([ref4[0], ref4[1]], axis=1)

    def grouped(mats, i, k, rhs):
        out = jnp.zeros((ROWS, 2 * LANES), F32)
        for g in range(PER):
            r = jnp.dot(mats[i, k * PER + g], rhs, preferred_element_type=F32)
            out = jnp.where(group_of == g, r, out)
        return out

    build_taps(0)
    wait_bytes(xs.at[0], load_sem.at[0])
    wait_bytes(gi.at[0], load_sem.at[1])
    acc[...] = jnp.zeros_like(acc)

    def prepare(k, carry):
        x = xs[0, k].astype(F32)
        acc[...] += x * x
        vs[0, k] = (gi[0, k].astype(F32) * x).astype(BF16)
        return carry

    lax.fori_loop(0, chunks, prepare, 0)

    pl.semaphore_wait(barrier, n - 1 + 3 * (nh - 1))

    share(0, True)

    @pl.when(has_next)
    def _():
        def send(k, carry):
            halo_fwd(0, k).start()
            return carry

        lax.fori_loop(0, chunks, send, 0)

    @pl.when(c == 0)
    def _():
        part[0:LAYERS, nh:] = jnp.zeros((LAYERS, nh, SEQS, ROWS), F32)

        def clear(k, carry):
            for i in range(LAYERS):
                vh[i, k] = jnp.zeros((SEQS, ROWS, LANES), BF16)
            return carry

        lax.fori_loop(0, chunks, clear, 0)

    @pl.when(c == n - 1)
    def _():
        def clear(k, carry):
            for i in range(LAYERS):
                gzx[i, k, :, ROWS:] = jnp.zeros((SEQS, ROWS, LANES), BF16)
            return carry

        lax.fori_loop(0, chunks, clear, 0)

    swap().start()
    if 0 in ARRIVE:
        send_arrive(ARRIVE.index(0))
    build_taps(1)
    for i in range(LAYERS):
        wait_bytes(go.at[i], load_sem.at[4 + i])
    for i in range(1, LAYERS):
        wait_bytes(gi.at[i], load_sem.at[1 + i])

    step = 2 if chunks % 2 == 0 else 1
    for i in range(LAYERS):
        if i == 1:
            build_taps(2)
        if i == 2:
            build_back(2)
        wait_own(i)

        @pl.when(has_prev)
        def _():
            wait_bytes(part.at[i, pl.ds(nh, nh)], pr2.at[i])

        own = inverse_of(shared(i, 0))
        before = inverse_of(shared(i, nh))
        for s in range(SEQS):
            bc[i, s] = column(own[s:s + 1])
            bcp[s] = column(before[s:s + 1])
        if i + 1 < LAYERS:
            acc[...] = jnp.zeros_like(acc)

        def forward_one(k):
            for s in range(SEQS):
                ux[i, k, s, 0:ROWS] = (vh[i, k, s].astype(F32) * bcp[s]).astype(BF16)
                ux[i, k, s, ROWS:] = (
                    gi[i, k, s].astype(F32) * (xs[i, k, s].astype(F32) * bc[i, s])).astype(BF16)
            z = grouped(taps, i, k, both(ux.at[i, k]))
            for s in range(SEQS):
                zs_part = z[:, s * LANES:(s + 1) * LANES]
                zs[i, k, s] = zs_part
                if i + 1 < LAYERS:
                    x_next = (go[i, k, s].astype(F32) * zs_part).astype(BF16)
                    xs[i + 1, k, s] = x_next
                    x_wide = x_next.astype(F32)
                    acc[s] += x_wide * x_wide
                    vs[i + 1, k, s] = (gi[i + 1, k, s].astype(F32) * x_wide).astype(BF16)

        def forward(q, carry):
            ks = [q * step + r for r in range(step)]

            @pl.when(has_prev)
            def _():
                for k in ks:
                    halo_fwd(i, k).wait_recv()

            for k in ks:
                forward_one(k)
            if i + 1 < LAYERS:
                @pl.when(has_next)
                def _():
                    for k in ks:
                        halo_fwd(i + 1, k).start()
            return carry

        lax.fori_loop(0, chunks // step, forward, 0)
        if i + 1 < LAYERS:
            share(i + 1, True)
            if i + 1 in ARRIVE:
                send_arrive(ARRIVE.index(i + 1))

    early = chunks // 2
    for i in reversed(range(LAYERS)):
        ph = LAYERS + i
        last = i == LAYERS - 1
        if not last:
            wait_own(LAYERS + i + 1)
            mean = shared(LAYERS + i + 1, 0) * (1.0 / (width * nh))
            for s in range(SEQS):
                bcp[s] = column(mean[s:s + 1]) * bc[i + 1, s]

        def enter(k, carry):
            if last:
                for b in range(2):
                    wait_bytes(g3.at[:, pl.ds(b * half, half), cols(k)], ar.at[b, k])
            for s in range(SEQS):
                if last:
                    g = g3[s, :, cols(k)].astype(F32)
                else:
                    g = (bc[i + 1, s] * (gn[k, s] - xs[i + 1, k, s].astype(F32) * bcp[s])).astype(BF16).astype(F32)
                gzx[i, k, s, 0:ROWS] = (go[i, k, s].astype(F32) * g).astype(BF16)
                ggo[i, k, s] = (g * zs[i, k, s]).astype(BF16)

            @pl.when(has_prev)
            def _():
                halo_bwd(i, k).start()

            pltpu.make_async_copy(ggo.at[i, k], ggo_out.at[i, :, :, cols(k)], out_sem.at[i]).start()
            return carry

        lax.fori_loop(0, chunks, enter, 0)

        if last:
            build_back(1)
            build_back(0)

        def diagonals(k, carry):
            grad = jnp.concatenate([gzx[i, k, 0, 0:ROWS], gzx[i, k, 1, 0:ROWS]], axis=1)
            turned = jnp.dot(flip, grad, preferred_element_type=F32).astype(BF16)
            rows = both(ux.at[i, k])
            lhs, rhs = [], []
            for t in range(tiles):
                tile = turned[ROWS - 16 * t - 16:ROWS - 16 * t]
                lhs.append(jnp.concatenate([tile] * PER, axis=0) * own_group)
                rhs.append(rows[16 * t:16 * t + ROWS + 16])
            prod = lax.dot_general(
                jnp.concatenate(lhs, axis=1), jnp.concatenate(rhs, axis=1),
                (((1,), (1,)), ((), ())), preferred_element_type=F32)
            tail = jnp.concatenate([prod[:, ROWS:], jnp.zeros((ROWS, LANES - 16), F32)], axis=1)
            merged = jnp.where(col + lax.rem(row, 16) > 15, prod[:, 0:LANES], tail)
            for g in range(PER):
                rolled = pltpu.roll(merged[16 * g:16 * g + 16], LANES - 15, 1, stride=1, stride_axis=0)
                lags[pl.ds(k * PER + g, 1), :] = jnp.sum(rolled, axis=0, keepdims=True)
            return carry

        lax.fori_loop(0, early, diagonals, 0)
        acc[...] = jnp.zeros_like(acc)

        def backward_one(k):
            gu = grouped(back, i, k, both(gzx.at[i, k]))
            for s in range(SEQS):
                gu_part = gu[:, s * LANES:(s + 1) * LANES]
                normed = xs[i, k, s].astype(F32) * bc[i, s]
                ggi[i, k, s] = (gu_part * normed).astype(BF16)
                gn_part = gu_part * gi[i, k, s].astype(F32)
                gn[k, s] = gn_part
                acc[s] += gn_part * normed

        def backward(q, carry):
            ks = [q * step + r for r in range(step)]

            @pl.when(has_next)
            def _():
                for k in ks:
                    halo_bwd(i, k).wait_recv()

            for k in ks:
                backward_one(k)
            for k in ks:
                pltpu.make_async_copy(ggi.at[i, k], ggi_out.at[i, :, :, cols(k)], out_sem.at[LAYERS + i]).start()
            return carry

        lax.fori_loop(0, chunks // step, backward, 0)
        share(ph, False)
        lax.fori_loop(early, chunks, diagonals, 0)
        per = ROWS // n
        peer_row = lax.broadcasted_iota(jnp.int32, (n, LANES), 0)
        peer_col = lax.broadcasted_iota(jnp.int32, (n, LANES), 1)
        pieces = []
        for q in range(per):
            pick = (lax.rem(peer_col + peer_row * per + q, ROWS) == 0).astype(F32)
            pieces.append(lax.dot_general(
                pick, lags[...], (((1,), (1,)), ((), ())), preferred_element_type=F32,
                precision=lax.Precision.HIGHEST))
        lines = jnp.concatenate(pieces, axis=1)
        span = lines.shape[1] // 2
        for p in range(n):
            for r in range(2):
                fsend[i, p, r:r + 1, :] = lines[p:p + 1, r * span:(r + 1) * span]
        frecv[i, c] = fsend[i, c]

        def send_lags(o, carry):
            lag_copy(i, o).start()
            return carry

        lax.fori_loop(1, n, send_lags, 0)

    wait_own(LAYERS)
    mean = shared(LAYERS, 0) * (1.0 / (width * nh))
    for s in range(SEQS):
        bcp[s] = column(mean[s:s + 1]) * bc[0, s]

    def finish(k, carry):
        for s in range(SEQS):
            g0[k, s] = (bc[0, s] * (gn[k, s] - xs[0, k, s].astype(F32) * bcp[s])).astype(BF16)
        for b in range(2):
            target, remote, local = leave(b, k)

            @pl.when(target != c)
            def _():
                remote.start()

            @pl.when(target == c)
            def _():
                local.start()
        return carry

    lax.fori_loop(0, chunks, finish, 0)

    for i in range(LAYERS):
        wait_bytes(frecv.at[i, pl.ds(0, n - 1)], fr.at[i])
        gf_out[i] = jnp.sum(frecv[i], axis=0)

    swap().wait_send()
    for i in range(LAYERS):
        wait_bytes(ggo.at[i], out_sem.at[i])
        wait_bytes(ggi.at[i], out_sem.at[LAYERS + i])
        wait_bytes(fsend.at[i, pl.ds(0, n - 1)], fs.at[i])
    for ph in range(2 * LAYERS):
        for o in range(1, nh):
            part_own(ph, o).wait_send()
    @pl.when(has_next)
    def _():
        for ph in range(LAYERS):
            for o in range(nh):
                part_next(ph, o).wait_send()

        def drain(k, carry):
            for i in range(LAYERS):
                halo_fwd(i, k).wait_send()
            return carry

        lax.fori_loop(0, chunks, drain, 0)

    @pl.when(has_prev)
    def _():
        def drain(k, carry):
            for i in range(LAYERS):
                halo_bwd(i, k).wait_send()
            return carry

        lax.fori_loop(0, chunks, drain, 0)

    def drain(k, carry):
        for b in range(2):
            for target, remote, local in (leave(b, k), arrive(b, k)):
                @pl.when(target != c)
                def _():
                    remote.wait_send()

            wait_bytes(gin_out.at[:, pl.ds(b * half, half), cols(k)], lr.at[b, k])
        return carry

    lax.fori_loop(0, chunks, drain, 0)


def hand_over(per, groups, a, b, c, d, a_out, b_out, c_out, d_out, held, get, put):
    pairs = [(a.at[s], a_out.at[s]) for s in range(SEQS)]
    for i in range(LAYERS):
        for s in range(SEQS):
            pairs += [(b.at[i, s], b_out.at[i, s]), (c.at[i, s], c_out.at[i, s])]
    for j, (src, _) in enumerate(pairs):
        pltpu.make_async_copy(src, held.at[j], get.at[j]).start()
    half = per // 2
    for i in range(LAYERS):
        for q in range(per):
            at = (q % half) * groups
            d_out[i, q:q + 1, :] = d[i, q // half:q // half + 1, at:at + groups]
    for j, (src, dst) in enumerate(pairs):
        pltpu.make_async_copy(src, held.at[j], get.at[j]).wait()
        pltpu.make_async_copy(held.at[j], dst, put.at[j]).start()
    for j, (src, dst) in enumerate(pairs):
        pltpu.make_async_copy(held.at[j], dst, put.at[j]).wait()


def local(n, nh, activations, grad_in, gate_out, gate_in, filters):
    width = activations.shape[2]
    chunks, groups = width // LANES, width // GROUP
    per = ROWS // n
    span = per * groups // 2
    block = (SEQS, ROWS, LANES)
    wide = (SEQS, 2 * ROWS, LANES)
    any_spec = pl.BlockSpec(memory_space=pl.ANY)
    vmem_spec = pl.BlockSpec(memory_space=pltpu.VMEM)
    dma = pltpu.SemaphoreType.DMA
    grad_input, ggo, ggi, lags = pl.pallas_call(
        functools.partial(kernel, n, nh, width),
        out_shape=(
            jax.ShapeDtypeStruct(activations.shape, BF16),
            jax.ShapeDtypeStruct(gate_out.shape, BF16),
            jax.ShapeDtypeStruct(gate_in.shape, BF16),
            jax.ShapeDtypeStruct((LAYERS, 2, span), F32),
        ),
        in_specs=[any_spec] * 4 + [vmem_spec],
        out_specs=(any_spec, any_spec, any_spec, vmem_spec),
        scratch_shapes=[
            pltpu.VMEM((LAYERS, chunks) + block, BF16),
            pltpu.VMEM((LAYERS, chunks) + block, BF16),
            pltpu.VMEM((LAYERS, chunks) + block, BF16),
            pltpu.VMEM((LAYERS, chunks) + block, BF16),
            pltpu.VMEM((LAYERS, chunks) + block, BF16),
            pltpu.VMEM((LAYERS, chunks) + wide, BF16),
            pltpu.VMEM((LAYERS, chunks) + block, F32),
            pltpu.VMEM((SEQS, ROWS, width), BF16),
            pltpu.VMEM((SEQS, ROWS // 2, width), BF16),
            pltpu.VMEM((LAYERS, chunks) + wide, BF16),
            pltpu.VMEM((chunks,) + block, F32),
            pltpu.VMEM((LAYERS, chunks) + block, BF16),
            pltpu.VMEM((LAYERS, chunks) + block, BF16),
            pltpu.VMEM((chunks,) + block, BF16),
            pltpu.VMEM((LAYERS, groups, ROWS, 2 * LANES), BF16),
            pltpu.VMEM((LAYERS, groups, ROWS, 2 * LANES), BF16),
            pltpu.VMEM((LAYERS, groups, LANES), F32),
            pltpu.VMEM((LAYERS, groups, LANES), F32),
            pltpu.VMEM((LAYERS,) + block, F32),
            pltpu.VMEM(block, F32),
            pltpu.VMEM(block, F32),
            pltpu.VMEM((2 * LAYERS, 2 * nh, SEQS, ROWS), F32),
            pltpu.VMEM((groups, LANES), F32),
            pltpu.VMEM((LAYERS, n, 2, span), F32),
            pltpu.VMEM((LAYERS, n, 2, span), F32),
            dma((7,)),
            dma((LAYERS, chunks)), dma((LAYERS, chunks)),
            dma((LAYERS, chunks)), dma((LAYERS, chunks)),
            dma((2 * LAYERS, 2 * nh)), dma((2 * LAYERS,)), dma((2 * LAYERS,)),
            dma((LAYERS,)), dma((LAYERS,)),
            dma((2, chunks)), dma((2, chunks)), dma((2,)),
            dma((2, chunks)), dma((2, chunks)),
            dma((2 * LAYERS,)),
        ],
        compiler_params=pltpu.CompilerParams(
            collective_id=0, has_side_effects=True, vmem_limit_bytes=64 * 1024 * 1024 - 65536),
    )(activations, grad_in, gate_out, gate_in, filters)
    grad_input, ggo, ggi, grad_filters = pl.pallas_call(
        functools.partial(hand_over, per, groups),
        out_shape=(
            jax.ShapeDtypeStruct(activations.shape, BF16),
            jax.ShapeDtypeStruct(gate_out.shape, BF16),
            jax.ShapeDtypeStruct(gate_in.shape, BF16),
            jax.ShapeDtypeStruct((LAYERS, per, groups), F32),
        ),
        in_specs=[any_spec] * 3 + [vmem_spec],
        out_specs=(any_spec, any_spec, any_spec, vmem_spec),
        scratch_shapes=[
            pltpu.VMEM((SEQS * (2 * LAYERS + 1),) + activations.shape[1:], BF16),
            dma((SEQS * (2 * LAYERS + 1),)), dma((SEQS * (2 * LAYERS + 1),)),
        ],
    )(grad_input, ggo, ggi, lags)
    return grad_input, ggo, ggi, grad_filters.transpose(0, 2, 1)


def solution(mesh):
    n, nh = mesh.shape["ctx"], mesh.shape["ch"]
    return jax.shard_map(
        functools.partial(local, n, nh),
        mesh=mesh,
        in_specs=(
            P(None, "ctx", "ch"),
            P(None, "ctx", "ch"),
            P(None, None, "ctx", "ch"),
            P(None, None, "ctx", "ch"),
            P(None, "ch", None),
        ),
        out_specs=(
            P(None, "ctx", "ch"),
            P(None, None, "ctx", "ch"),
            P(None, None, "ctx", "ch"),
            P(None, "ch", "ctx"),
        ),
        check_vma=False,
    )
```
